512 devices in a mesh: lang: 64 (over y, z), rep: 8 (over x, core).
Axes of the slice: x: 4, y: 8, z: 8, core: 2. Of those that a mesh axis runs over, the one named last changes fastest.
Arguments:
- tokens: bfloat16 [65536, 1024], P(('lang', 'rep')), may hold values from -24 to 24
- grad_out: bfloat16 [65536, 1024], P(('lang', 'rep')), may hold values from -24 to 24
- lang_ids: int32 [65536], P(('lang', 'rep')), may hold values from 0 to 7, as said below
- slot_ids: int32 [65536], P(('lang', 'rep')), may hold values from 0 to 23, as said below
- w_up: bfloat16 [1024, 32768], P(None, 'lang'), may hold values from -0.1875 to 0.1875
- w_down_t: bfloat16 [1024, 32768], P(None, 'lang'), may hold values from -0.09375 to 0.09375
Outputs:
- ffn_out: bfloat16 [65536, 1024], P(('lang', 'rep'))
- grad_tokens: bfloat16 [65536, 1024], P(('lang', 'rep'))
- grad_up: float32 [1024, 32768], P('rep', 'lang')
- grad_down: float32 [1024, 32768], P('rep', 'lang')
The draws below stay inside these ranges and needn't reach their ends.
Inputs may be any that keep to these rules, and one draw needn't show every extreme that they name: `lang_ids`: each device holds 128 consecutive tokens. On every device one language, the same on all devices, has exactly 24 tokens; every other language has at most 18 tokens on a device, and on every device one of them has exactly 18. `slot_ids`: on each device the tokens of one language hold the distinct slots 0 to their count minus 1, in no particular order.
All inputs are finite; a program needn't handle non-finite values.
Results may differ from the reference program's by a relative error of at most 0.0058.
Values may be sent and summed in bfloat16 or wider, within the bound.
A program may use at most 128 MiB of HBM per device.

```python
import jax
import jax.numpy as jnp
from jax import lax

D = 1024
HIDDEN_SIZE = 4096
MODULES = 8
TOK_DEV = 128
CAPACITY = 18
HOT = 24
TOKENS = 65536
N_LANG = 64


def routing(key):
    block_count = TOKENS // TOK_DEV
    hot_lang = jax.random.randint(jax.random.fold_in(key, 101), (), 0, MODULES).astype(jnp.int32)
    spread = TOK_DEV // 128
    remain = TOK_DEV - HOT - CAPACITY

    def one_block(block_key):
        key_jitter, key_langs, key_place, key_slots = jax.random.split(block_key, 4)
        jitter = jax.random.randint(key_jitter, (MODULES - 3,), -spread, spread + 1)
        cut_points = remain * jnp.arange(1, MODULES - 2) // (MODULES - 2) + jitter
        positions = jnp.arange(remain)
        ranked = 1 + jnp.sum(positions[:, None] >= cut_points[None, :], axis=1)
        ranked = jnp.concatenate([jnp.zeros((CAPACITY,), jnp.int32), ranked.astype(jnp.int32)])
        others = (hot_lang + 1 + jax.random.permutation(key_langs, MODULES - 1)) % MODULES
        rest_ids = jnp.take(others, ranked).astype(jnp.int32)
        ordered = jnp.concatenate([jnp.full((HOT,), hot_lang, jnp.int32), rest_ids])
        scores = jax.random.permutation(key_slots, TOK_DEV)
        same_lang = ordered[:, None] == ordered[None, :]
        slot_list = jnp.sum(same_lang & (scores[None, :] < scores[:, None]), axis=1).astype(jnp.int32)
        placing = jax.random.permutation(key_place, TOK_DEV)
        lang_row = jnp.zeros((TOK_DEV,), jnp.int32).at[placing].set(ordered)
        slot_row = jnp.zeros((TOK_DEV,), jnp.int32).at[placing].set(slot_list)
        return (lang_row, slot_row)

    def block_key_of(block_index):
        return jax.random.fold_in(key, block_index + 1000)
    block_keys = jax.vmap(block_key_of)(jnp.arange(block_count))
    lang_rows, slot_rows = jax.vmap(one_block)(block_keys)
    return (lang_rows.reshape(-1), slot_rows.reshape(-1))


def draw_lang_ids(key, part):
    return routing(key)[0]


def draw_slot_ids(key, part):
    return routing(key)[1]


def spiked(array, key, source, target, blocks, factor):
    def block_of(dim):
        return (jnp.arange(array.shape[dim]) // (array.shape[dim] // blocks)).reshape((-1,) + (1,) * (array.ndim - 1 - dim))

    near = jax.random.permutation(key, blocks)[block_of(target)]
    other_side = (block_of(target) + blocks // 2) % blocks
    return jnp.where((block_of(source) == near) | (block_of(source) == other_side), factor * array, array)


def steps_of(key, dims, pieces, least, largest):
    factor_of = 1.0
    for dim, blocks in pieces:
        draws = jax.random.uniform(jax.random.fold_in(jax.random.fold_in(key, 6), dim), (blocks,), jnp.float32, least / len(pieces), largest / len(pieces))
        factor_of = factor_of * jnp.repeat(jnp.exp(draws), dims[dim] // blocks).reshape((-1,) + (1,) * (len(dims) - 1 - dim))
    return factor_of


def noise(stream_key, dims, scale, most, cuts=(), kind=jnp.bfloat16):
    entries = scale * jax.random.normal(stream_key, dims, jnp.float32)
    if cuts:
        entries = entries * steps_of(stream_key, dims, cuts, -0.22, 0.18)
    return jnp.clip(entries, -most, most).astype(kind)


def heavy_noise(rng, dims, scale, most, pieces, heavy, kind=jnp.bfloat16):
    array = scale * jax.random.normal(rng, dims, jnp.float32)
    if pieces:
        array = array * steps_of(rng, dims, pieces, -0.22, 0.18)
    return jnp.clip(spiked(array, jax.random.fold_in(rng, 3), *heavy), -most, most).astype(kind)


def setup_inputs(seed: int = 0) -> dict:
    arg_keys = jax.random.split(jax.random.key(seed), 7)
    tokens = heavy_noise(arg_keys[0], (TOKENS, D), 1.0, 24.0, ((0, 512),), (0, 1, 512, 6.0))
    grad_out = heavy_noise(arg_keys[1], (TOKENS, D), 1.0, 24.0, ((0, 512),), (0, 1, 512, 6.0))
    lang_ids = draw_lang_ids(jax.random.fold_in(arg_keys[6], 71), 0)
    slot_ids = draw_slot_ids(jax.random.fold_in(arg_keys[6], 71), 0)
    w_up = noise(arg_keys[4], (D, MODULES * HIDDEN_SIZE), D ** -0.5, 0.1875, ((1, 64),))
    w_down_t = noise(arg_keys[5], (D, MODULES * HIDDEN_SIZE), HIDDEN_SIZE ** -0.5, 0.09375, ((1, 64),))
    return dict(tokens=tokens, grad_out=grad_out, lang_ids=lang_ids, slot_ids=slot_ids, w_up=w_up, w_down_t=w_down_t)


INV_ROOT_TWO = 0.7071067811865476
INV_ROOT_TAU = 0.3989422804014327


def gelu_value(values):
    return 0.5 * values * (1.0 + lax.erf(values * INV_ROOT_TWO))


def gelu_slope(values):
    return 0.5 * (1.0 + lax.erf(values * INV_ROOT_TWO)) + values * jnp.exp(-0.5 * values * values) * INV_ROOT_TAU


def reference(tokens, grad_out, lang_ids, slot_ids, w_up, w_down_t):
    groups = N_LANG // MODULES
    block_units = HIDDEN_SIZE // groups
    block_count = TOKENS // TOK_DEV
    keep_mask = slot_ids < CAPACITY
    target = jnp.where(keep_mask, lang_ids * CAPACITY + slot_ids, MODULES * CAPACITY).astype(jnp.int32)
    places = target.reshape(block_count, TOK_DEV)

    def place_one(block_vals, block_index):
        return jnp.zeros((MODULES * CAPACITY, D), block_vals.dtype).at[block_index].set(block_vals, mode="drop")

    def dispatch(values):
        filled = jax.vmap(place_one)(values.reshape(block_count, TOK_DEV, D), places)
        filled = filled.reshape(block_count, MODULES, CAPACITY, D).transpose(1, 0, 2, 3)
        return filled.reshape(MODULES, block_count * CAPACITY, D)

    up_stack = w_up.reshape(D, MODULES, HIDDEN_SIZE).transpose(1, 0, 2)
    down_stack = w_down_t.reshape(D, MODULES, HIDDEN_SIZE).transpose(1, 0, 2)

    def module_step(operands):
        module_x, module_dy, weight_up, weight_down = operands
        pre_act = jnp.dot(module_x, weight_up, preferred_element_type=jnp.float32)
        hidden = gelu_value(pre_act).astype(jnp.bfloat16)
        d_hidden = jnp.dot(module_dy, weight_down, preferred_element_type=jnp.float32)
        d_pre = (d_hidden * gelu_slope(pre_act)).astype(jnp.bfloat16)
        out_sum = jnp.zeros((module_x.shape[0], D), jnp.float32)
        dx_sum = jnp.zeros((module_x.shape[0], D), jnp.float32)
        for block_index in range(groups):
            low_unit = block_index * block_units
            high_unit = low_unit + block_units
            part_out = jnp.dot(hidden[:, low_unit:high_unit], weight_down[:, low_unit:high_unit].T, preferred_element_type=jnp.float32).astype(jnp.bfloat16)
            part_dx = jnp.dot(d_pre[:, low_unit:high_unit], weight_up[:, low_unit:high_unit].T, preferred_element_type=jnp.float32).astype(jnp.bfloat16)
            part_out = lax.optimization_barrier(part_out)
            part_dx = lax.optimization_barrier(part_dx)
            out_sum = out_sum + part_out.astype(jnp.float32)
            dx_sum = dx_sum + part_dx.astype(jnp.float32)
        grad_down = jnp.dot(module_dy.T, hidden, preferred_element_type=jnp.float32) * (1.0 / TOK_DEV)
        grad_up = jnp.dot(module_x.T, d_pre, preferred_element_type=jnp.float32) * (1.0 / TOK_DEV)
        return out_sum.astype(jnp.bfloat16), dx_sum.astype(jnp.bfloat16), grad_up, grad_down

    results = lax.map(module_step, (dispatch(tokens), dispatch(grad_out), up_stack, down_stack))
    safe_index = jnp.minimum(target, MODULES * CAPACITY - 1).astype(jnp.int32).reshape(block_count, TOK_DEV)

    def take_rows(all_rows, row_index):
        return jnp.take(all_rows, row_index, axis=0)

    def undispatch(per_module):
        filled = per_module.reshape(MODULES, block_count, CAPACITY, D).transpose(1, 0, 2, 3)
        filled = filled.reshape(block_count, MODULES * CAPACITY, D)
        picked = jax.vmap(take_rows)(filled, safe_index).reshape(TOKENS, D)
        return jnp.where(keep_mask[:, None], picked, jnp.zeros_like(picked))

    ffn_out = undispatch(results[0])
    grad_tokens = undispatch(results[1])
    grad_up = results[2].transpose(1, 0, 2).reshape(D, MODULES * HIDDEN_SIZE)
    grad_down = results[3].transpose(1, 0, 2).reshape(D, MODULES * HIDDEN_SIZE)
    return ffn_out, grad_tokens, grad_up, grad_down
```

```python
import jax
import jax.numpy as jnp
from jax import lax
from jax.sharding import Mesh
from jax.sharding import PartitionSpec as P

MODULES = 8
TOK_DEV = 128
CAPACITY = 18


INV_ROOT_TWO = 0.7071067811865476
INV_ROOT_TAU = 0.3989422804014327


def gelu_value(values):
    return 0.5 * values * (1.0 + lax.erf(values * INV_ROOT_TWO))


def gelu_slope(values):
    return (
        0.5 * (1.0 + lax.erf(values * INV_ROOT_TWO))
        + values * jnp.exp(-0.5 * values * values) * INV_ROOT_TAU
    )


def per_device(tokens, grad_out, lang_ids, slot_ids, w_up, w_down_t):
    feature_width = tokens.shape[1]
    capacity = CAPACITY
    keep_mask = slot_ids < capacity
    target = jnp.where(keep_mask, lang_ids * capacity + slot_ids, MODULES * capacity)
    safe_slot = jnp.minimum(slot_ids, capacity - 1)
    token_scale = 1.0 / TOK_DEV

    def place(values):
        buffer = (
            jnp.zeros((MODULES * capacity, feature_width), values.dtype)
            .at[target]
            .set(values, mode="drop")
        )
        return buffer.reshape(MODULES, capacity, feature_width)

    def dispatch(values):
        by_y = lax.all_to_all(place(values), "ly", split_axis=0, concat_axis=0, tiled=True)
        every = lax.all_gather(by_y, "lz", axis=0, tiled=True)
        return every.reshape(-1, feature_width)

    def give_back(rows):
        parts = rows.astype(jnp.float32).reshape(-1, capacity, feature_width)
        summed = lax.psum_scatter(parts, "lz", scatter_dimension=0, tiled=True)
        summed = summed.astype(jnp.bfloat16)
        return lax.all_to_all(summed, "ly", split_axis=0, concat_axis=0, tiled=True)

    def collect(returned):
        picked = returned[lang_ids, safe_slot]
        return jnp.where(keep_mask[:, None], picked, jnp.zeros_like(picked))

    flat_tokens = dispatch(tokens)
    flat_grads = dispatch(grad_out)
    pre_flat = jnp.dot(flat_tokens, w_up, preferred_element_type=jnp.float32)
    hidden_flat = gelu_value(pre_flat).astype(jnp.bfloat16)
    partial_rows = lax.dot_general(
        hidden_flat, w_down_t, (((1,), (1,)), ((), ())), preferred_element_type=jnp.float32
    ).astype(jnp.bfloat16)
    returned = give_back(partial_rows)
    grad_down = lax.psum_scatter(
        lax.dot_general(
            flat_grads, hidden_flat, (((0,), (0,)), ((), ())), preferred_element_type=jnp.float32
        )
        * token_scale,
        "rep",
        scatter_dimension=0,
        tiled=True,
    )
    d_hidden = jnp.dot(flat_grads, w_down_t, preferred_element_type=jnp.float32)
    d_pre = (d_hidden * gelu_slope(pre_flat)).astype(jnp.bfloat16)
    grad_up = lax.psum_scatter(
        lax.dot_general(
            flat_tokens, d_pre, (((0,), (0,)), ((), ())), preferred_element_type=jnp.float32
        )
        * token_scale,
        "rep",
        scatter_dimension=0,
        tiled=True,
    )
    dx_part = lax.dot_general(
        d_pre, w_up, (((1,), (1,)), ((), ())), preferred_element_type=jnp.float32
    ).astype(jnp.bfloat16)
    dx_back = give_back(dx_part)
    return (collect(returned), collect(dx_back), grad_up, grad_down)


def solution(mesh):
    n_lang = mesh.shape["lang"]
    groups = n_lang // MODULES
    devices = mesh.devices.reshape(MODULES, groups, mesh.shape["rep"])
    split_mesh = Mesh(devices, ("ly", "lz", "rep"))
    rows = P(("ly", "lz", "rep"), None)
    ids = P(("ly", "lz", "rep"))
    cols = P(None, ("ly", "lz"))
    return jax.shard_map(
        per_device,
        mesh=split_mesh,
        in_specs=(rows, rows, ids, ids, cols, cols),
        out_specs=(rows, rows, P("rep", ("ly", "lz")), P("rep", ("ly", "lz"))),
        check_vma=False,
    )
```

```python
import functools

import jax
import jax.numpy as jnp
from jax import lax
from jax.experimental import pallas as pl
from jax.experimental.pallas import tpu as pltpu
from jax.sharding import Mesh
from jax.sharding import PartitionSpec as P

MODULES = 8
TOK_DEV = 128
CAPACITY = 18


INV_ROOT_TWO = 0.7071067811865476
INV_ROOT_TAU = 0.3989422804014327


def gelu_value(values):
    return 0.5 * values * (1.0 + lax.erf(values * INV_ROOT_TWO))


def gelu_slope(values):
    return (
        0.5 * (1.0 + lax.erf(values * INV_ROOT_TWO))
        + values * jnp.exp(-0.5 * values * values) * INV_ROOT_TAU
    )

MESH_IDS = pl.DeviceIdType.MESH
VMEM_LIMIT = 48 * 1024 * 1024


def enter(n):
    me = lax.axis_index("lz")
    right, left = lax.rem(me + 1, n), lax.rem(me + n - 1, n)
    barrier = pltpu.get_barrier_semaphore()
    for neighbour in (left, right):
        pl.semaphore_signal(barrier, inc=1, device_id={"lz": neighbour}, device_id_type=MESH_IDS)
    pl.semaphore_wait(barrier, 2)
    return me, right, left


def ring_gather_kernel(n, x_ref, o_ref, send_sem, recv_sem):
    me, right, left = enter(n)
    o_ref[0, me] = x_ref[0]
    o_ref[1, me] = x_ref[1]
    copies = []
    for step in range(n - 1):
        going_right = lax.rem(me - step + n, n)
        going_left = lax.rem(me + step, n)
        src_r = x_ref.at[0] if step == 0 else o_ref.at[0, going_right]
        src_l = x_ref.at[1] if step == 0 else o_ref.at[1, going_left]
        to_right = pltpu.make_async_remote_copy(
            src_ref=src_r, dst_ref=o_ref.at[0, going_right],
            send_sem=send_sem.at[0, step], recv_sem=recv_sem.at[0, step],
            device_id={"lz": right}, device_id_type=MESH_IDS)
        to_left = pltpu.make_async_remote_copy(
            src_ref=src_l, dst_ref=o_ref.at[1, going_left],
            send_sem=send_sem.at[1, step], recv_sem=recv_sem.at[1, step],
            device_id={"lz": left}, device_id_type=MESH_IDS)
        to_right.start()
        to_left.start()
        to_right.wait_recv()
        to_left.wait_recv()
        copies += [to_right, to_left]
    for copy in copies:
        copy.wait_send()


def ring_gather(x, n):
    two, rows, width = x.shape
    return pl.pallas_call(
        functools.partial(ring_gather_kernel, n),
        out_shape=jax.ShapeDtypeStruct((two, n, rows, width), x.dtype),
        in_specs=[pl.BlockSpec(memory_space=pltpu.VMEM)],
        out_specs=pl.BlockSpec(memory_space=pltpu.VMEM),
        scratch_shapes=[pltpu.SemaphoreType.DMA((2, n - 1)), pltpu.SemaphoreType.DMA((2, n - 1))],
        compiler_params=pltpu.CompilerParams(
            collective_id=0, has_side_effects=True, vmem_limit_bytes=VMEM_LIMIT),
    )(x)


def ring_sum_kernel(n, pa_ref, pb_ref, o_ref, send_r, send_l, recv_r, recv_l, send_sem, recv_sem):
    me, right, left = enter(n)
    copies = []
    for step in range(n - 1):
        for_right = lax.rem(me + 2 * n - 1 - step, n)
        for_left = lax.rem(me + 1 + step, n)
        if step == 0:
            send_r[0] = pa_ref[for_right].astype(jnp.float32)
            send_l[0] = pb_ref[for_left].astype(jnp.float32)
        else:
            copies[-2].wait_recv()
            copies[-1].wait_recv()
            send_r[step] = recv_r[step - 1] + pa_ref[for_right].astype(jnp.float32)
            send_l[step] = recv_l[step - 1] + pb_ref[for_left].astype(jnp.float32)
        to_right = pltpu.make_async_remote_copy(
            src_ref=send_r.at[step], dst_ref=recv_r.at[step],
            send_sem=send_sem.at[0, step], recv_sem=recv_sem.at[0, step],
            device_id={"lz": right}, device_id_type=MESH_IDS)
        to_left = pltpu.make_async_remote_copy(
            src_ref=send_l.at[step], dst_ref=recv_l.at[step],
            send_sem=send_sem.at[1, step], recv_sem=recv_sem.at[1, step],
            device_id={"lz": left}, device_id_type=MESH_IDS)
        to_right.start()
        to_left.start()
        copies += [to_right, to_left]
    copies[-2].wait_recv()
    copies[-1].wait_recv()
    o_ref[0] = (recv_r[n - 2] + pa_ref[me].astype(jnp.float32)).astype(o_ref.dtype)
    o_ref[1] = (recv_l[n - 2] + pb_ref[me].astype(jnp.float32)).astype(o_ref.dtype)
    for copy in copies:
        copy.wait_send()


def ring_sum(first, second, n):
    _, rows, width = first.shape
    return pl.pallas_call(
        functools.partial(ring_sum_kernel, n),
        out_shape=jax.ShapeDtypeStruct((2, rows, width), first.dtype),
        in_specs=[pl.BlockSpec(memory_space=pltpu.VMEM)] * 2,
        out_specs=pl.BlockSpec(memory_space=pltpu.VMEM),
        scratch_shapes=[pltpu.VMEM((n - 1, rows, width), jnp.float32)] * 4
        + [pltpu.SemaphoreType.DMA((2, n - 1)), pltpu.SemaphoreType.DMA((2, n - 1))],
        compiler_params=pltpu.CompilerParams(
            collective_id=1, has_side_effects=True, vmem_limit_bytes=VMEM_LIMIT),
    )(first, second)


def per_device(tokens, grad_out, lang_ids, slot_ids, w_up, w_down_t):
    feature_width = tokens.shape[1]
    capacity = CAPACITY
    keep_mask = slot_ids < capacity
    target = jnp.where(keep_mask, lang_ids * capacity + slot_ids, MODULES * capacity)
    safe_slot = jnp.minimum(slot_ids, capacity - 1)
    token_scale = 1.0 / TOK_DEV

    def place(values):
        buffer = (
            jnp.zeros((MODULES * capacity, feature_width), values.dtype)
            .at[target]
            .set(values, mode="drop")
        )
        return buffer.reshape(MODULES, capacity, feature_width)

    n_z = lax.axis_size("lz")

    def dispatch(first, second):
        both = jnp.stack([place(first), place(second)])
        by_y = lax.all_to_all(both, "ly", split_axis=1, concat_axis=1, tiled=True)
        every = ring_gather(by_y.reshape(2, -1, feature_width), n_z)
        every = every.reshape(2, -1, feature_width)
        return every[0], every[1]

    def give_back(first, second):
        summed = ring_sum(
            first.reshape(n_z, -1, feature_width), second.reshape(n_z, -1, feature_width), n_z)
        summed = summed.reshape(2, -1, capacity, feature_width)
        back = lax.all_to_all(summed, "ly", split_axis=1, concat_axis=1, tiled=True)
        return back[0], back[1]

    def collect(returned):
        picked = returned[lang_ids, safe_slot]
        return jnp.where(keep_mask[:, None], picked, jnp.zeros_like(picked))

    flat_tokens, flat_grads = dispatch(tokens, grad_out)
    pre_flat = jnp.dot(flat_tokens, w_up, preferred_element_type=jnp.float32)
    hidden_flat = gelu_value(pre_flat).astype(jnp.bfloat16)
    partial_rows = lax.dot_general(
        hidden_flat, w_down_t, (((1,), (1,)), ((), ())), preferred_element_type=jnp.float32
    ).astype(jnp.bfloat16)
    grad_down = lax.psum_scatter(
        lax.dot_general(
            flat_grads, hidden_flat, (((0,), (0,)), ((), ())), preferred_element_type=jnp.float32
        )
        * token_scale,
        "rep",
        scatter_dimension=0,
        tiled=True,
    )
    d_hidden = jnp.dot(flat_grads, w_down_t, preferred_element_type=jnp.float32)
    d_pre = (d_hidden * gelu_slope(pre_flat)).astype(jnp.bfloat16)
    grad_up = lax.psum_scatter(
        lax.dot_general(
            flat_tokens, d_pre, (((0,), (0,)), ((), ())), preferred_element_type=jnp.float32
        )
        * token_scale,
        "rep",
        scatter_dimension=0,
        tiled=True,
    )
    dx_part = lax.dot_general(
        d_pre, w_up, (((1,), (1,)), ((), ())), preferred_element_type=jnp.float32
    ).astype(jnp.bfloat16)
    returned, dx_back = give_back(partial_rows, dx_part)
    return (collect(returned), collect(dx_back), grad_up, grad_down)


def solution(mesh):
    n_lang = mesh.shape["lang"]
    groups = n_lang // MODULES
    devices = mesh.devices.reshape(MODULES, groups, mesh.shape["rep"])
    split_mesh = Mesh(devices, ("ly", "lz", "rep"))
    rows = P(("ly", "lz", "rep"), None)
    ids = P(("ly", "lz", "rep"))
    cols = P(None, ("ly", "lz"))
    return jax.shard_map(
        per_device,
        mesh=split_mesh,
        in_specs=(rows, rows, ids, ids, cols, cols),
        out_specs=(rows, rows, P("rep", ("ly", "lz")), P("rep", ("ly", "lz"))),
        check_vma=False,
    )
```

```python
import functools

import jax
import jax.numpy as jnp
from jax import lax
from jax.experimental import pallas as pl
from jax.experimental.pallas import tpu as pltpu
from jax.sharding import Mesh
from jax.sharding import PartitionSpec as P

MODULES = 8
TOK_DEV = 128
CAPACITY = 18


INV_ROOT_TWO = 0.7071067811865476
INV_ROOT_TAU = 0.3989422804014327


def gelu_value(values):
    return 0.5 * values * (1.0 + lax.erf(values * INV_ROOT_TWO))


def gelu_slope(values):
    return (
        0.5 * (1.0 + lax.erf(values * INV_ROOT_TWO))
        + values * jnp.exp(-0.5 * values * values) * INV_ROOT_TAU
    )

MESH_IDS = pl.DeviceIdType.MESH
VMEM_LIMIT = 48 * 1024 * 1024
PARTS = 3


def enter(n):
    me = lax.axis_index("lz")
    right, left = lax.rem(me + 1, n), lax.rem(me + n - 1, n)
    barrier = pltpu.get_barrier_semaphore()
    for neighbour in (left, right):
        pl.semaphore_signal(barrier, inc=1, device_id={"lz": neighbour}, device_id_type=MESH_IDS)
    pl.semaphore_wait(barrier, 2)
    return me, right, left


def ring_gather_kernel(n, x_ref, o_ref, send_sem, recv_sem):
    me, right, left = enter(n)
    half = x_ref.shape[1] // PARTS
    o_ref[0, me] = x_ref[0]
    o_ref[1, me] = x_ref[1]

    def hop(stream, part, step):
        rows = pl.ds(part * half, half)
        if stream == 0:
            slot, peer = lax.rem(me - step + n, n), right
        else:
            slot, peer = lax.rem(me + step, n), left
        src = x_ref.at[stream, rows] if step == 0 else o_ref.at[stream, slot, rows]
        return pltpu.make_async_remote_copy(
            src_ref=src, dst_ref=o_ref.at[stream, slot, rows],
            send_sem=send_sem.at[stream, part, step], recv_sem=recv_sem.at[stream, part, step],
            device_id={"lz": peer}, device_id_type=MESH_IDS)

    order = [(stream, part) for part in range(PARTS) for stream in range(2)]
    copies = []
    last = {}
    for key in order:
        last[key] = hop(*key, 0)
        last[key].start()
        copies.append(last[key])
    for step in range(1, n - 1):
        for key in order:
            last[key].wait_recv()
            last[key] = hop(*key, step)
            last[key].start()
            copies.append(last[key])
    for key in order:
        last[key].wait_recv()
    for copy in copies:
        copy.wait_send()


def ring_gather(x, n):
    two, rows, width = x.shape
    return pl.pallas_call(
        functools.partial(ring_gather_kernel, n),
        out_shape=jax.ShapeDtypeStruct((two, n, rows, width), x.dtype),
        in_specs=[pl.BlockSpec(memory_space=pltpu.VMEM)],
        out_specs=pl.BlockSpec(memory_space=pltpu.VMEM),
        scratch_shapes=[pltpu.SemaphoreType.DMA((2, PARTS, n - 1)), pltpu.SemaphoreType.DMA((2, PARTS, n - 1))],
        compiler_params=pltpu.CompilerParams(
            collective_id=0, has_side_effects=True, vmem_limit_bytes=VMEM_LIMIT),
    )(x)


def ring_sum_kernel(n, pa_ref, pb_ref, o_ref, first_r, first_l, send_r, send_l, recv_r, recv_l,
                    send_sem, recv_sem):
    me, right, left = enter(n)
    half = pa_ref.shape[1] // PARTS
    parts = (pa_ref, pb_ref)
    sends = (send_r, send_l)
    recvs = (recv_r, recv_l)

    def chunk_for(stream, step):
        if stream == 0:
            return lax.rem(me + 2 * n - 1 - step, n)
        return lax.rem(me + 1 + step, n)

    firsts = (first_r, first_l)

    def hop(stream, part, step):
        rows = pl.ds(part * half, half)
        if step == 0:
            src = parts[stream].at[chunk_for(stream, 0), rows]
            dst = firsts[stream].at[rows]
        else:
            src, dst = sends[stream].at[step, rows], recvs[stream].at[step, rows]
        return pltpu.make_async_remote_copy(
            src_ref=src, dst_ref=dst,
            send_sem=send_sem.at[stream, part, step], recv_sem=recv_sem.at[stream, part, step],
            device_id={"lz": right if stream == 0 else left}, device_id_type=MESH_IDS)

    order = [(stream, part) for part in range(PARTS) for stream in range(2)]
    copies = []
    last = {}
    for stream, part in order:
        last[stream, part] = hop(stream, part, 0)
        last[stream, part].start()
        copies.append(last[stream, part])
    for step in range(1, n - 1):
        for stream, part in order:
            rows = pl.ds(part * half, half)
            last[stream, part].wait_recv()
            if step == 1:
                came = firsts[stream][rows].astype(jnp.float32)
            else:
                came = recvs[stream][step - 1, rows]
            sends[stream][step, rows] = came + parts[stream][chunk_for(stream, step), rows].astype(
                jnp.float32)
            last[stream, part] = hop(stream, part, step)
            last[stream, part].start()
            copies.append(last[stream, part])
    for stream, part in order:
        rows = pl.ds(part * half, half)
        last[stream, part].wait_recv()
        o_ref[stream, rows] = (
            recvs[stream][n - 2, rows] + parts[stream][me, rows].astype(jnp.float32)
        ).astype(o_ref.dtype)
    for copy in copies:
        copy.wait_send()


def ring_sum(first, second, n):
    _, rows, width = first.shape
    return pl.pallas_call(
        functools.partial(ring_sum_kernel, n),
        out_shape=jax.ShapeDtypeStruct((2, rows, width), first.dtype),
        in_specs=[pl.BlockSpec(memory_space=pltpu.VMEM)] * 2,
        out_specs=pl.BlockSpec(memory_space=pltpu.VMEM),
        scratch_shapes=[pltpu.VMEM((rows, width), first.dtype)] * 2
        + [pltpu.VMEM((n - 1, rows, width), jnp.float32)] * 4
        + [pltpu.SemaphoreType.DMA((2, PARTS, n - 1)), pltpu.SemaphoreType.DMA((2, PARTS, n - 1))],
        compiler_params=pltpu.CompilerParams(
            collective_id=1, has_side_effects=True, vmem_limit_bytes=VMEM_LIMIT),
    )(first, second)


def y_exchange_kernel(n_y, x_ref, o_ref, send_sem, recv_sem):
    me = lax.axis_index("ly")
    barrier = pltpu.get_barrier_semaphore()
    for k in range(1, n_y):
        pl.semaphore_signal(
            barrier, inc=1, device_id={"ly": lax.rem(me + k, n_y)}, device_id_type=MESH_IDS)
    pl.semaphore_wait(barrier, n_y - 1)

    def exchange(k, src, dst):
        return pltpu.make_async_remote_copy(
            src_ref=src, dst_ref=dst, send_sem=send_sem.at[k], recv_sem=recv_sem.at[k],
            device_id={"ly": lax.rem(me + k, n_y)}, device_id_type=MESH_IDS)

    copies = []
    for k in range(1, n_y):
        copy = exchange(k, x_ref.at[:, lax.rem(me + k, n_y)], o_ref.at[:, me])
        copy.start()
        copies.append(copy)
    o_ref[:, me] = x_ref[:, me]
    for k in range(1, n_y):
        exchange(k, x_ref.at[:, me], o_ref.at[:, lax.rem(me + n_y - k, n_y)]).wait_recv()
    for copy in copies:
        copy.wait_send()


def y_exchange(x, call_id):
    n_y = x.shape[1]
    return pl.pallas_call(
        functools.partial(y_exchange_kernel, n_y),
        out_shape=jax.ShapeDtypeStruct(x.shape, x.dtype),
        in_specs=[pl.BlockSpec(memory_space=pltpu.VMEM)],
        out_specs=pl.BlockSpec(memory_space=pltpu.VMEM),
        scratch_shapes=[pltpu.SemaphoreType.DMA((n_y,)), pltpu.SemaphoreType.DMA((n_y,))],
        compiler_params=pltpu.CompilerParams(
            collective_id=call_id, has_side_effects=True, vmem_limit_bytes=VMEM_LIMIT),
    )(x)


def per_device(tokens, grad_out, lang_ids, slot_ids, w_up, w_down_t):
    feature_width = tokens.shape[1]
    capacity = CAPACITY
    keep_mask = slot_ids < capacity
    target = jnp.where(keep_mask, lang_ids * capacity + slot_ids, MODULES * capacity)
    safe_slot = jnp.minimum(slot_ids, capacity - 1)
    token_scale = 1.0 / TOK_DEV

    def place(values):
        buffer = (
            jnp.zeros((MODULES * capacity, feature_width), values.dtype)
            .at[target]
            .set(values, mode="drop")
        )
        return buffer.reshape(MODULES, capacity, feature_width)

    n_z = lax.axis_size("lz")

    def dispatch(first, second):
        both = jnp.stack([place(first), place(second)])
        lanes = 128
        by_y = y_exchange(both.reshape(2, MODULES, -1, lanes), 2)
        every = ring_gather(by_y.reshape(2, -1, feature_width), n_z)
        every = every.reshape(2, -1, feature_width)
        return every[0], every[1]

    def give_back(first, second):
        summed = ring_sum(
            first.reshape(n_z, -1, feature_width), second.reshape(n_z, -1, feature_width), n_z)
        summed = summed.reshape(2, -1, capacity, feature_width)
        back = y_exchange(summed.reshape(2, MODULES, -1, 128), 3)
        back = back.reshape(2, MODULES, capacity, feature_width)
        return back[0], back[1]

    def collect(returned):
        picked = returned[lang_ids, safe_slot]
        return jnp.where(keep_mask[:, None], picked, jnp.zeros_like(picked))

    flat_tokens, flat_grads = dispatch(tokens, grad_out)
    pre_flat = jnp.dot(flat_tokens, w_up, preferred_element_type=jnp.float32)
    hidden_flat = gelu_value(pre_flat).astype(jnp.bfloat16)
    partial_rows = lax.dot_general(
        hidden_flat, w_down_t, (((1,), (1,)), ((), ())), preferred_element_type=jnp.float32
    ).astype(jnp.bfloat16)
    grad_down = lax.psum_scatter(
        lax.dot_general(
            flat_grads, hidden_flat, (((0,), (0,)), ((), ())), preferred_element_type=jnp.float32
        )
        * token_scale,
        "rep",
        scatter_dimension=0,
        tiled=True,
    )
    d_hidden = jnp.dot(flat_grads, w_down_t, preferred_element_type=jnp.float32)
    d_pre = (d_hidden * gelu_slope(pre_flat)).astype(jnp.bfloat16)
    grad_up = lax.psum_scatter(
        lax.dot_general(
            flat_tokens, d_pre, (((0,), (0,)), ((), ())), preferred_element_type=jnp.float32
        )
        * token_scale,
        "rep",
        scatter_dimension=0,
        tiled=True,
    )
    dx_part = lax.dot_general(
        d_pre, w_up, (((1,), (1,)), ((), ())), preferred_element_type=jnp.float32
    ).astype(jnp.bfloat16)
    returned, dx_back = give_back(partial_rows, dx_part)
    return (collect(returned), collect(dx_back), grad_up, grad_down)


def solution(mesh):
    n_lang = mesh.shape["lang"]
    groups = n_lang // MODULES
    devices = mesh.devices.reshape(MODULES, groups, mesh.shape["rep"])
    split_mesh = Mesh(devices, ("ly", "lz", "rep"))
    rows = P(("ly", "lz", "rep"), None)
    ids = P(("ly", "lz", "rep"))
    cols = P(None, ("ly", "lz"))
    return jax.shard_map(
        per_device,
        mesh=split_mesh,
        in_specs=(rows, rows, ids, ids, cols, cols),
        out_specs=(rows, rows, P("rep", ("ly", "lz")), P("rep", ("ly", "lz"))),
        check_vma=False,
    )
```

```python
import functools

import jax
import jax.numpy as jnp
from jax import lax
from jax.experimental import pallas as pl
from jax.experimental.pallas import tpu as pltpu
from jax.sharding import Mesh
from jax.sharding import PartitionSpec as P

MODULES = 8
TOK_DEV = 128
CAPACITY = 18


INV_ROOT_TWO = 0.7071067811865476
INV_ROOT_TAU = 0.3989422804014327


def gelu_value(values):
    return 0.5 * values * (1.0 + lax.erf(values * INV_ROOT_TWO))


def gelu_slope(values):
    return (
        0.5 * (1.0 + lax.erf(values * INV_ROOT_TWO))
        + values * jnp.exp(-0.5 * values * values) * INV_ROOT_TAU
    )

MESH_IDS = pl.DeviceIdType.MESH
VMEM_LIMIT = 60 * 1024 * 1024
PARTS = 3


def enter(n, others=()):
    me = lax.axis_index("lz")
    right, left = lax.rem(me + 1, n), lax.rem(me + n - 1, n)
    peers = [("lz", left), ("lz", right)] + list(others)
    barrier = pltpu.get_barrier_semaphore()
    for axis, neighbour in peers:
        pl.semaphore_signal(barrier, inc=1, device_id={axis: neighbour}, device_id_type=MESH_IDS)
    pl.semaphore_wait(barrier, len(peers))
    return me, right, left


def rep_ring(n_r):
    rep = lax.axis_index("rep")
    chips = n_r // 2
    x, core = rep // 2, lax.rem(rep, 2)
    pos = core * (x + 1) + (1 - core) * lax.rem(n_r - x, n_r)

    def rep_at(p):
        p = lax.rem(p + 2 * n_r, n_r)
        up = 1 - lax.rem(p + n_r - 1, n_r) // chips
        return 2 * (up * (p - 1) + (1 - up) * lax.rem(n_r - p, n_r)) + up

    return pos, rep_at


def ring_gather_kernel(n, x_ref, o_ref, send_sem, recv_sem):
    me, right, left = enter(n)
    half = x_ref.shape[1] // PARTS
    o_ref[0, me] = x_ref[0]
    o_ref[1, me] = x_ref[1]

    def hop(stream, part, step):
        rows = pl.ds(part * half, half)
        if stream == 0:
            slot, peer = lax.rem(me - step + n, n), right
        else:
            slot, peer = lax.rem(me + step, n), left
        src = x_ref.at[stream, rows] if step == 0 else o_ref.at[stream, slot, rows]
        return pltpu.make_async_remote_copy(
            src_ref=src, dst_ref=o_ref.at[stream, slot, rows],
            send_sem=send_sem.at[stream, part, step], recv_sem=recv_sem.at[stream, part, step],
            device_id={"lz": peer}, device_id_type=MESH_IDS)

    order = [(stream, part) for part in range(PARTS) for stream in range(2)]
    copies = []
    last = {}
    for key in order:
        last[key] = hop(*key, 0)
        last[key].start()
        copies.append(last[key])
    for step in range(1, n - 1):
        for key in order:
            last[key].wait_recv()
            last[key] = hop(*key, step)
            last[key].start()
            copies.append(last[key])
    for key in order:
        last[key].wait_recv()
    for copy in copies:
        copy.wait_send()


def ring_gather(x, n):
    two, rows, width = x.shape
    return pl.pallas_call(
        functools.partial(ring_gather_kernel, n),
        out_shape=jax.ShapeDtypeStruct((two, n, rows, width), x.dtype),
        in_specs=[pl.BlockSpec(memory_space=pltpu.VMEM)],
        out_specs=pl.BlockSpec(memory_space=pltpu.VMEM),
        scratch_shapes=[pltpu.SemaphoreType.DMA((2, PARTS, n - 1)), pltpu.SemaphoreType.DMA((2, PARTS, n - 1))],
        compiler_params=pltpu.CompilerParams(
            collective_id=0, has_side_effects=True, vmem_limit_bytes=VMEM_LIMIT),
    )(x)


def ring_sum_kernel(n, n_r, pa_ref, pb_ref, gd_ref, gu_ref, o_ref, od_ref, ou_ref, first_r, first_l,
                    send_r, send_l, recv_r, recv_l, send_sem, recv_sem,
                    gsend_f, gsend_b, grecv_f, grecv_b, gsend_sem, grecv_sem):
    pos, rep_at = rep_ring(n_r)
    ahead, behind = rep_at(pos + 1), rep_at(pos - 1)
    me, right, left = enter(n, [("rep", ahead), ("rep", behind)])
    block = od_ref.shape[0]
    grads = (gd_ref, gu_ref)
    gsends = (gsend_f, gsend_b)
    grecvs = (grecv_f, grecv_b)

    def grad_rows(stream, step):
        dest = pos - 1 - step if stream == 0 else pos + 1 + step
        return pl.ds(pl.multiple_of(rep_at(dest) * block, block), block)

    def grad_hop(stream, step):
        if step == 0:
            src = grads[stream].at[grad_rows(stream, 0)]
        else:
            src = gsends[stream].at[step]
        return pltpu.make_async_remote_copy(
            src_ref=src, dst_ref=grecvs[stream].at[step],
            send_sem=gsend_sem.at[stream, step], recv_sem=grecv_sem.at[stream, step],
            device_id={"rep": ahead if stream == 0 else behind}, device_id_type=MESH_IDS)

    grad_copies = []
    grad_last = {}

    def grad_step(step):
        for stream in range(2):
            if step > 0:
                grad_last[stream].wait_recv()
                gsends[stream][step] = grecvs[stream][step - 1] + grads[stream][grad_rows(stream, step)]
            grad_last[stream] = grad_hop(stream, step)
            grad_last[stream].start()
            grad_copies.append(grad_last[stream])

    half = pa_ref.shape[1] // PARTS
    parts = (pa_ref, pb_ref)
    sends = (send_r, send_l)
    recvs = (recv_r, recv_l)

    def chunk_for(stream, step):
        if stream == 0:
            return lax.rem(me + 2 * n - 1 - step, n)
        return lax.rem(me + 1 + step, n)

    firsts = (first_r, first_l)

    def hop(stream, part, step):
        rows = pl.ds(part * half, half)
        if step == 0:
            src = parts[stream].at[chunk_for(stream, 0), rows]
            dst = firsts[stream].at[rows]
        else:
            src, dst = sends[stream].at[step, rows], recvs[stream].at[step, rows]
        return pltpu.make_async_remote_copy(
            src_ref=src, dst_ref=dst,
            send_sem=send_sem.at[stream, part, step], recv_sem=recv_sem.at[stream, part, step],
            device_id={"lz": right if stream == 0 else left}, device_id_type=MESH_IDS)

    order = [(stream, part) for part in range(PARTS) for stream in range(2)]
    copies = []
    last = {}
    for stream, part in order:
        last[stream, part] = hop(stream, part, 0)
        last[stream, part].start()
        copies.append(last[stream, part])
    grad_step(0)
    for step in range(1, max(n, n_r) - 1):
        if step < n_r - 1:
            grad_step(step)
        if step >= n - 1:
            continue
        for stream, part in order:
            rows = pl.ds(part * half, half)
            last[stream, part].wait_recv()
            if step == 1:
                came = firsts[stream][rows].astype(jnp.float32)
            else:
                came = recvs[stream][step - 1, rows]
            sends[stream][step, rows] = came + parts[stream][chunk_for(stream, step), rows].astype(
                jnp.float32)
            last[stream, part] = hop(stream, part, step)
            last[stream, part].start()
            copies.append(last[stream, part])
    for stream, part in order:
        rows = pl.ds(part * half, half)
        last[stream, part].wait_recv()
        o_ref[stream, rows] = (
            recvs[stream][n - 2, rows] + parts[stream][me, rows].astype(jnp.float32)
        ).astype(o_ref.dtype)
    own = pl.ds(pl.multiple_of(rep_at(pos) * block, block), block)
    for stream, out in ((0, od_ref), (1, ou_ref)):
        grad_last[stream].wait_recv()
        out[...] = grecvs[stream][n_r - 2] + grads[stream][own]
    for copy in copies + grad_copies:
        copy.wait_send()


def ring_sum(first, second, grad_d, grad_u, n, n_r):
    _, rows, width = first.shape
    d_rows, d_cols = grad_d.shape
    block = d_rows // n_r
    return pl.pallas_call(
        functools.partial(ring_sum_kernel, n, n_r),
        out_shape=(
            jax.ShapeDtypeStruct((2, rows, width), first.dtype),
            jax.ShapeDtypeStruct((block, d_cols), grad_d.dtype),
            jax.ShapeDtypeStruct((block, d_cols), grad_u.dtype),
        ),
        in_specs=[pl.BlockSpec(memory_space=pltpu.VMEM)] * 4,
        out_specs=[pl.BlockSpec(memory_space=pltpu.VMEM)] * 3,
        scratch_shapes=[pltpu.VMEM((rows, width), first.dtype)] * 2
        + [pltpu.VMEM((n - 1, rows, width), jnp.float32)] * 4
        + [pltpu.SemaphoreType.DMA((2, PARTS, n - 1)), pltpu.SemaphoreType.DMA((2, PARTS, n - 1))]
        + [pltpu.VMEM((n_r - 1, block, d_cols), jnp.float32)] * 4
        + [pltpu.SemaphoreType.DMA((2, n_r - 1)), pltpu.SemaphoreType.DMA((2, n_r - 1))],
        compiler_params=pltpu.CompilerParams(
            collective_id=1, has_side_effects=True, vmem_limit_bytes=VMEM_LIMIT),
    )(first, second, grad_d, grad_u)


def y_exchange_kernel(n_y, x_ref, o_ref, send_sem, recv_sem):
    me = lax.axis_index("ly")
    barrier = pltpu.get_barrier_semaphore()
    for k in range(1, n_y):
        pl.semaphore_signal(
            barrier, inc=1, device_id={"ly": lax.rem(me + k, n_y)}, device_id_type=MESH_IDS)
    pl.semaphore_wait(barrier, n_y - 1)

    def exchange(k, src, dst):
        return pltpu.make_async_remote_copy(
            src_ref=src, dst_ref=dst, send_sem=send_sem.at[k], recv_sem=recv_sem.at[k],
            device_id={"ly": lax.rem(me + k, n_y)}, device_id_type=MESH_IDS)

    copies = []
    for k in range(1, n_y):
        copy = exchange(k, x_ref.at[:, lax.rem(me + k, n_y)], o_ref.at[:, me])
        copy.start()
        copies.append(copy)
    o_ref[:, me] = x_ref[:, me]
    for k in range(1, n_y):
        exchange(k, x_ref.at[:, me], o_ref.at[:, lax.rem(me + n_y - k, n_y)]).wait_recv()
    for copy in copies:
        copy.wait_send()


def y_exchange(x, call_id):
    n_y = x.shape[1]
    return pl.pallas_call(
        functools.partial(y_exchange_kernel, n_y),
        out_shape=jax.ShapeDtypeStruct(x.shape, x.dtype),
        in_specs=[pl.BlockSpec(memory_space=pltpu.VMEM)],
        out_specs=pl.BlockSpec(memory_space=pltpu.VMEM),
        scratch_shapes=[pltpu.SemaphoreType.DMA((n_y,)), pltpu.SemaphoreType.DMA((n_y,))],
        compiler_params=pltpu.CompilerParams(
            collective_id=call_id, has_side_effects=True, vmem_limit_bytes=VMEM_LIMIT),
    )(x)


def per_device(tokens, grad_out, lang_ids, slot_ids, w_up, w_down_t):
    feature_width = tokens.shape[1]
    capacity = CAPACITY
    keep_mask = slot_ids < capacity
    target = jnp.where(keep_mask, lang_ids * capacity + slot_ids, MODULES * capacity)
    safe_slot = jnp.minimum(slot_ids, capacity - 1)
    token_scale = 1.0 / TOK_DEV

    def place(values):
        buffer = (
            jnp.zeros((MODULES * capacity, feature_width), values.dtype)
            .at[target]
            .set(values, mode="drop")
        )
        return buffer.reshape(MODULES, capacity, feature_width)

    n_z = lax.axis_size("lz")

    def dispatch(first, second):
        both = jnp.stack([place(first), place(second)])
        lanes = 128
        by_y = y_exchange(both.reshape(2, MODULES, -1, lanes), 2)
        every = ring_gather(by_y.reshape(2, -1, feature_width), n_z)
        every = every.reshape(2, -1, feature_width)
        return every[0], every[1]

    def give_back(first, second, grad_d, grad_u):
        summed, grad_d, grad_u = ring_sum(
            first.reshape(n_z, -1, feature_width), second.reshape(n_z, -1, feature_width),
            grad_d, grad_u, n_z, lax.axis_size("rep"))
        summed = summed.reshape(2, -1, capacity, feature_width)
        back = y_exchange(summed.reshape(2, MODULES, -1, 128), 3)
        back = back.reshape(2, MODULES, capacity, feature_width)
        return back[0], back[1], grad_d, grad_u

    def collect(returned):
        picked = returned[lang_ids, safe_slot]
        return jnp.where(keep_mask[:, None], picked, jnp.zeros_like(picked))

    flat_tokens, flat_grads = dispatch(tokens, grad_out)
    pre_flat = jnp.dot(flat_tokens, w_up, preferred_element_type=jnp.float32)
    hidden_flat = gelu_value(pre_flat).astype(jnp.bfloat16)
    partial_rows = lax.dot_general(
        hidden_flat, w_down_t, (((1,), (1,)), ((), ())), preferred_element_type=jnp.float32
    ).astype(jnp.bfloat16)
    grad_down = lax.dot_general(
        flat_grads, hidden_flat, (((0,), (0,)), ((), ())), preferred_element_type=jnp.float32
    ) * token_scale
    d_hidden = jnp.dot(flat_grads, w_down_t, preferred_element_type=jnp.float32)
    d_pre = (d_hidden * gelu_slope(pre_flat)).astype(jnp.bfloat16)
    grad_up = lax.dot_general(
        flat_tokens, d_pre, (((0,), (0,)), ((), ())), preferred_element_type=jnp.float32
    ) * token_scale
    dx_part = lax.dot_general(
        d_pre, w_up, (((1,), (1,)), ((), ())), preferred_element_type=jnp.float32
    ).astype(jnp.bfloat16)
    returned, dx_back, grad_down, grad_up = give_back(partial_rows, dx_part, grad_down, grad_up)
    return (collect(returned), collect(dx_back), grad_up, grad_down)


def solution(mesh):
    n_lang = mesh.shape["lang"]
    groups = n_lang // MODULES
    devices = mesh.devices.reshape(MODULES, groups, mesh.shape["rep"])
    split_mesh = Mesh(devices, ("ly", "lz", "rep"))
    rows = P(("ly", "lz", "rep"), None)
    ids = P(("ly", "lz", "rep"))
    cols = P(None, ("ly", "lz"))
    return jax.shard_map(
        per_device,
        mesh=split_mesh,
        in_specs=(rows, rows, ids, ids, cols, cols),
        out_specs=(rows, rows, P("rep", ("ly", "lz")), P("rep", ("ly", "lz"))),
        check_vma=False,
    )
```

```python
import functools

import jax
import jax.numpy as jnp
from jax import lax
from jax.experimental import pallas as pl
from jax.experimental.pallas import tpu as pltpu
from jax.sharding import Mesh
from jax.sharding import PartitionSpec as P

MODULES = 8
TOK_DEV = 128
CAPACITY = 18


INV_ROOT_TWO = 0.7071067811865476
INV_ROOT_TAU = 0.3989422804014327


def gelu_value(values):
    return 0.5 * values * (1.0 + lax.erf(values * INV_ROOT_TWO))


def gelu_slope(values):
    return (
        0.5 * (1.0 + lax.erf(values * INV_ROOT_TWO))
        + values * jnp.exp(-0.5 * values * values) * INV_ROOT_TAU
    )

MESH_IDS = pl.DeviceIdType.MESH
MIB = 1024 * 1024
PARTS = 3


def enter(n, others=()):
    me = lax.axis_index("lz")
    right, left = lax.rem(me + 1, n), lax.rem(me + n - 1, n)
    peers = [("lz", left), ("lz", right)] + list(others)
    barrier = pltpu.get_barrier_semaphore()
    for axis, neighbour in peers:
        pl.semaphore_signal(barrier, inc=1, device_id={axis: neighbour}, device_id_type=MESH_IDS)
    pl.semaphore_wait(barrier, len(peers))
    return me, right, left


def rep_ring(n_r):
    rep = lax.axis_index("rep")
    chips = n_r // 2
    x, core = rep // 2, lax.rem(rep, 2)
    pos = core * (x + 1) + (1 - core) * lax.rem(n_r - x, n_r)

    def rep_at(p):
        p = lax.rem(p + 2 * n_r, n_r)
        up = 1 - lax.rem(p + n_r - 1, n_r) // chips
        return 2 * (up * (p - 1) + (1 - up) * lax.rem(n_r - p, n_r)) + up

    return pos, rep_at


def ring_gather_kernel(n, x_ref, o_ref, send_sem, recv_sem):
    me, right, left = enter(n)
    half = x_ref.shape[1] // PARTS
    o_ref[0, me] = x_ref[0]
    o_ref[1, me] = x_ref[1]

    def hop(stream, part, step):
        rows = pl.ds(part * half, half)
        if stream == 0:
            slot, peer = lax.rem(me - step + n, n), right
        else:
            slot, peer = lax.rem(me + step, n), left
        src = x_ref.at[stream, rows] if step == 0 else o_ref.at[stream, slot, rows]
        return pltpu.make_async_remote_copy(
            src_ref=src, dst_ref=o_ref.at[stream, slot, rows],
            send_sem=send_sem.at[stream, part, step], recv_sem=recv_sem.at[stream, part, step],
            device_id={"lz": peer}, device_id_type=MESH_IDS)

    order = [(stream, part) for part in range(PARTS) for stream in range(2)]
    copies = []
    last = {}
    for key in order:
        last[key] = hop(*key, 0)
        last[key].start()
        copies.append(last[key])
    for step in range(1, n - 1):
        for key in order:
            last[key].wait_recv()
            last[key] = hop(*key, step)
            last[key].start()
            copies.append(last[key])
    for key in order:
        last[key].wait_recv()
    for copy in copies:
        copy.wait_send()


def ring_gather(x, n):
    two, rows, width = x.shape
    return pl.pallas_call(
        functools.partial(ring_gather_kernel, n),
        out_shape=jax.ShapeDtypeStruct((two, n, rows, width), x.dtype),
        in_specs=[pl.BlockSpec(memory_space=pltpu.VMEM)],
        out_specs=pl.BlockSpec(memory_space=pltpu.VMEM),
        scratch_shapes=[pltpu.SemaphoreType.DMA((2, PARTS, n - 1)), pltpu.SemaphoreType.DMA((2, PARTS, n - 1))],
        compiler_params=pltpu.CompilerParams(
            collective_id=0, has_side_effects=True, vmem_limit_bytes=16 * MIB),
    )(x)


def ring_sum_kernel(n, n_r, pa_ref, pb_ref, gd_ref, gu_ref, o_ref, od_ref, ou_ref, first_r, first_l,
                    send_r, send_l, recv_r, recv_l, send_sem, recv_sem,
                    gsend_f, gsend_b, grecv_f, grecv_b, gsend_sem, grecv_sem):
    pos, rep_at = rep_ring(n_r)
    ahead, behind = rep_at(pos + 1), rep_at(pos - 1)
    me, right, left = enter(n, [("rep", ahead), ("rep", behind)])
    block = od_ref.shape[0]
    grads = (gd_ref, gu_ref)
    gsends = (gsend_f, gsend_b)
    grecvs = (grecv_f, grecv_b)

    def grad_rows(stream, step):
        dest = pos - 1 - step if stream == 0 else pos + 1 + step
        return pl.ds(pl.multiple_of(rep_at(dest) * block, block), block)

    def grad_hop(stream, step):
        if step == 0:
            src = grads[stream].at[grad_rows(stream, 0)]
        else:
            src = gsends[stream].at[step]
        return pltpu.make_async_remote_copy(
            src_ref=src, dst_ref=grecvs[stream].at[step],
            send_sem=gsend_sem.at[stream, step], recv_sem=grecv_sem.at[stream, step],
            device_id={"rep": ahead if stream == 0 else behind}, device_id_type=MESH_IDS)

    grad_copies = []
    grad_last = {}

    def grad_step(step):
        for stream in range(2):
            if step > 0:
                grad_last[stream].wait_recv()
                gsends[stream][step] = grecvs[stream][step - 1] + grads[stream][grad_rows(stream, step)]
            grad_last[stream] = grad_hop(stream, step)
            grad_last[stream].start()
            grad_copies.append(grad_last[stream])

    half = pa_ref.shape[1] // PARTS
    parts = (pa_ref, pb_ref)
    sends = (send_r, send_l)
    recvs = (recv_r, recv_l)

    def chunk_for(stream, step):
        if stream == 0:
            return lax.rem(me + 2 * n - 1 - step, n)
        return lax.rem(me + 1 + step, n)

    firsts = (first_r, first_l)

    def hop(stream, part, step):
        rows = pl.ds(part * half, half)
        if step == 0:
            src = parts[stream].at[chunk_for(stream, 0), rows]
            dst = firsts[stream].at[rows]
        else:
            src, dst = sends[stream].at[step, rows], recvs[stream].at[step, rows]
        return pltpu.make_async_remote_copy(
            src_ref=src, dst_ref=dst,
            send_sem=send_sem.at[stream, part, step], recv_sem=recv_sem.at[stream, part, step],
            device_id={"lz": right if stream == 0 else left}, device_id_type=MESH_IDS)

    order = [(stream, part) for part in range(PARTS) for stream in range(2)]
    copies = []
    last = {}
    for stream, part in order:
        last[stream, part] = hop(stream, part, 0)
        last[stream, part].start()
        copies.append(last[stream, part])
    grad_step(0)
    for step in range(1, max(n, n_r) - 1):
        if step < n_r - 1:
            grad_step(step)
        if step >= n - 1:
            continue
        for stream, part in order:
            rows = pl.ds(part * half, half)
            last[stream, part].wait_recv()
            if step == 1:
                came = firsts[stream][rows].astype(jnp.float32)
            else:
                came = recvs[stream][step - 1, rows]
            sends[stream][step, rows] = came + parts[stream][chunk_for(stream, step), rows].astype(
                jnp.float32)
            last[stream, part] = hop(stream, part, step)
            last[stream, part].start()
            copies.append(last[stream, part])
    for stream, part in order:
        rows = pl.ds(part * half, half)
        last[stream, part].wait_recv()
        o_ref[stream, rows] = (
            recvs[stream][n - 2, rows] + parts[stream][me, rows].astype(jnp.float32)
        ).astype(o_ref.dtype)
    own = pl.ds(pl.multiple_of(rep_at(pos) * block, block), block)
    for stream, out in ((0, od_ref), (1, ou_ref)):
        grad_last[stream].wait_recv()
        out[...] = grecvs[stream][n_r - 2] + grads[stream][own]
    for copy in copies + grad_copies:
        copy.wait_send()


def ring_sum(first, second, grad_d, grad_u, n, n_r):
    _, rows, width = first.shape
    d_rows, d_cols = grad_d.shape
    block = d_rows // n_r
    return pl.pallas_call(
        functools.partial(ring_sum_kernel, n, n_r),
        out_shape=(
            jax.ShapeDtypeStruct((2, rows, width), first.dtype),
            jax.ShapeDtypeStruct((block, d_cols), grad_d.dtype),
            jax.ShapeDtypeStruct((block, d_cols), grad_u.dtype),
        ),
        in_specs=[pl.BlockSpec(memory_space=pltpu.VMEM)] * 4,
        out_specs=[pl.BlockSpec(memory_space=pltpu.VMEM)] * 3,
        scratch_shapes=[pltpu.VMEM((rows, width), first.dtype)] * 2
        + [pltpu.VMEM((n - 1, rows, width), jnp.float32)] * 4
        + [pltpu.SemaphoreType.DMA((2, PARTS, n - 1)), pltpu.SemaphoreType.DMA((2, PARTS, n - 1))]
        + [pltpu.VMEM((n_r - 1, block, d_cols), jnp.float32)] * 4
        + [pltpu.SemaphoreType.DMA((2, n_r - 1)), pltpu.SemaphoreType.DMA((2, n_r - 1))],
        compiler_params=pltpu.CompilerParams(
            collective_id=1, has_side_effects=True, vmem_limit_bytes=44 * MIB),
    )(first, second, grad_d, grad_u)


def y_exchange_kernel(n_y, x_ref, o_ref, send_sem, recv_sem):
    me = lax.axis_index("ly")
    barrier = pltpu.get_barrier_semaphore()
    for k in range(1, n_y):
        pl.semaphore_signal(
            barrier, inc=1, device_id={"ly": lax.rem(me + k, n_y)}, device_id_type=MESH_IDS)
    pl.semaphore_wait(barrier, n_y - 1)

    def exchange(k, src, dst):
        return pltpu.make_async_remote_copy(
            src_ref=src, dst_ref=dst, send_sem=send_sem.at[k], recv_sem=recv_sem.at[k],
            device_id={"ly": lax.rem(me + k, n_y)}, device_id_type=MESH_IDS)

    copies = []
    for k in range(1, n_y):
        copy = exchange(k, x_ref.at[:, lax.rem(me + k, n_y)], o_ref.at[:, me])
        copy.start()
        copies.append(copy)
    o_ref[:, me] = x_ref[:, me]
    for k in range(1, n_y):
        exchange(k, x_ref.at[:, me], o_ref.at[:, lax.rem(me + n_y - k, n_y)]).wait_recv()
    for copy in copies:
        copy.wait_send()


def y_exchange(x, call_id):
    n_y = x.shape[1]
    return pl.pallas_call(
        functools.partial(y_exchange_kernel, n_y),
        out_shape=jax.ShapeDtypeStruct(x.shape, x.dtype),
        in_specs=[pl.BlockSpec(memory_space=pltpu.VMEM)],
        out_specs=pl.BlockSpec(memory_space=pltpu.VMEM),
        scratch_shapes=[pltpu.SemaphoreType.DMA((n_y,)), pltpu.SemaphoreType.DMA((n_y,))],
        compiler_params=pltpu.CompilerParams(
            collective_id=call_id, has_side_effects=True, vmem_limit_bytes=8 * MIB),
    )(x)


def per_device(tokens, grad_out, lang_ids, slot_ids, w_up, w_down_t):
    feature_width = tokens.shape[1]
    capacity = CAPACITY
    keep_mask = slot_ids < capacity
    target = jnp.where(keep_mask, lang_ids * capacity + slot_ids, MODULES * capacity)
    safe_slot = jnp.minimum(slot_ids, capacity - 1)
    token_scale = 1.0 / TOK_DEV

    def place(values):
        buffer = (
            jnp.zeros((MODULES * capacity, feature_width), values.dtype)
            .at[target]
            .set(values, mode="drop")
        )
        return buffer.reshape(MODULES, capacity, feature_width)

    n_z = lax.axis_size("lz")

    def dispatch(first, second):
        both = jnp.stack([place(first), place(second)])
        lanes = 128
        by_y = y_exchange(both.reshape(2, MODULES, -1, lanes), 2)
        every = ring_gather(by_y.reshape(2, -1, feature_width), n_z)
        every = every.reshape(2, -1, feature_width)
        return every[0], every[1]

    def give_back(first, second, grad_d, grad_u):
        summed, grad_d, grad_u = ring_sum(
            first.reshape(n_z, -1, feature_width), second.reshape(n_z, -1, feature_width),
            grad_d, grad_u, n_z, lax.axis_size("rep"))
        summed = summed.reshape(2, -1, capacity, feature_width)
        back = y_exchange(summed.reshape(2, MODULES, -1, 128), 3)
        back = back.reshape(2, MODULES, capacity, feature_width)
        return back[0], back[1], grad_d, grad_u

    def collect(returned):
        picked = returned[lang_ids, safe_slot]
        return jnp.where(keep_mask[:, None], picked, jnp.zeros_like(picked))

    flat_tokens, flat_grads = dispatch(tokens, grad_out)
    pre_flat = jnp.dot(flat_tokens, w_up, preferred_element_type=jnp.float32)
    hidden_flat = gelu_value(pre_flat).astype(jnp.bfloat16)
    partial_rows = lax.dot_general(
        hidden_flat, w_down_t, (((1,), (1,)), ((), ())), preferred_element_type=jnp.float32
    ).astype(jnp.bfloat16)
    grad_down = lax.dot_general(
        flat_grads, hidden_flat, (((0,), (0,)), ((), ())), preferred_element_type=jnp.float32
    ) * token_scale
    d_hidden = jnp.dot(flat_grads, w_down_t, preferred_element_type=jnp.float32)
    d_pre = (d_hidden * gelu_slope(pre_flat)).astype(jnp.bfloat16)
    grad_up = lax.dot_general(
        flat_tokens, d_pre, (((0,), (0,)), ((), ())), preferred_element_type=jnp.float32
    ) * token_scale
    dx_part = lax.dot_general(
        d_pre, w_up, (((1,), (1,)), ((), ())), preferred_element_type=jnp.float32
    ).astype(jnp.bfloat16)
    returned, dx_back, grad_down, grad_up = give_back(partial_rows, dx_part, grad_down, grad_up)
    return (collect(returned), collect(dx_back), grad_up, grad_down)


def solution(mesh):
    n_lang = mesh.shape["lang"]
    groups = n_lang // MODULES
    devices = mesh.devices.reshape(MODULES, groups, mesh.shape["rep"])
    split_mesh = Mesh(devices, ("ly", "lz", "rep"))
    rows = P(("ly", "lz", "rep"), None)
    ids = P(("ly", "lz", "rep"))
    cols = P(None, ("ly", "lz"))
    return jax.shard_map(
        per_device,
        mesh=split_mesh,
        in_specs=(rows, rows, ids, ids, cols, cols),
        out_specs=(rows, rows, P("rep", ("ly", "lz")), P("rep", ("ly", "lz"))),
        check_vma=False,
    )
```

```python
import functools

import jax
import jax.numpy as jnp
from jax import lax
from jax.experimental import pallas as pl
from jax.experimental.pallas import tpu as pltpu
from jax.sharding import Mesh
from jax.sharding import PartitionSpec as P

MODULES = 8
TOK_DEV = 128
CAPACITY = 18


INV_ROOT_TWO = 0.7071067811865476
INV_ROOT_TAU = 0.3989422804014327


def gelu_value(values):
    return 0.5 * values * (1.0 + lax.erf(values * INV_ROOT_TWO))


def gelu_slope(values):
    return (
        0.5 * (1.0 + lax.erf(values * INV_ROOT_TWO))
        + values * jnp.exp(-0.5 * values * values) * INV_ROOT_TAU
    )

MESH_IDS = pl.DeviceIdType.MESH
MIB = 1024 * 1024
PARTS = 3


def enter(n, others=()):
    me = lax.axis_index("lz")
    right, left = lax.rem(me + 1, n), lax.rem(me + n - 1, n)
    peers = [("lz", left), ("lz", right)] + list(others)
    barrier = pltpu.get_barrier_semaphore()
    for axis, neighbour in peers:
        pl.semaphore_signal(barrier, inc=1, device_id={axis: neighbour}, device_id_type=MESH_IDS)
    pl.semaphore_wait(barrier, len(peers))
    return me, right, left


def rep_ring(n_r):
    rep = lax.axis_index("rep")
    chips = n_r // 2
    x, core = rep // 2, lax.rem(rep, 2)
    pos = core * (x + 1) + (1 - core) * lax.rem(n_r - x, n_r)

    def rep_at(p):
        p = lax.rem(p + 2 * n_r, n_r)
        up = 1 - lax.rem(p + n_r - 1, n_r) // chips
        return 2 * (up * (p - 1) + (1 - up) * lax.rem(n_r - p, n_r)) + up

    return pos, rep_at


def ring_gather_kernel(n, x_ref, o_ref, send_sem, recv_sem):
    me, right, left = enter(n)
    half = x_ref.shape[1] // PARTS
    o_ref[0, me] = x_ref[0]
    o_ref[1, me] = x_ref[1]

    def hop(stream, part, step):
        rows = pl.ds(part * half, half)
        if stream == 0:
            slot, peer = lax.rem(me - step + n, n), right
        else:
            slot, peer = lax.rem(me + step, n), left
        src = x_ref.at[stream, rows] if step == 0 else o_ref.at[stream, slot, rows]
        return pltpu.make_async_remote_copy(
            src_ref=src, dst_ref=o_ref.at[stream, slot, rows],
            send_sem=send_sem.at[stream, part, step], recv_sem=recv_sem.at[stream, part, step],
            device_id={"lz": peer}, device_id_type=MESH_IDS)

    order = [(stream, part) for part in range(PARTS) for stream in range(2)]
    copies = []
    last = {}
    for key in order:
        last[key] = hop(*key, 0)
        last[key].start()
        copies.append(last[key])
    for step in range(1, n - 1):
        for key in order:
            last[key].wait_recv()
            last[key] = hop(*key, step)
            last[key].start()
            copies.append(last[key])
    for key in order:
        last[key].wait_recv()
    for copy in copies:
        copy.wait_send()


def ring_gather(x, n):
    two, rows, width = x.shape
    return pl.pallas_call(
        functools.partial(ring_gather_kernel, n),
        out_shape=jax.ShapeDtypeStruct((two, n, rows, width), x.dtype),
        in_specs=[pl.BlockSpec(memory_space=pltpu.VMEM)],
        out_specs=pl.BlockSpec(memory_space=pltpu.VMEM),
        scratch_shapes=[pltpu.SemaphoreType.DMA((2, PARTS, n - 1)), pltpu.SemaphoreType.DMA((2, PARTS, n - 1))],
        compiler_params=pltpu.CompilerParams(
            collective_id=0, has_side_effects=True, vmem_limit_bytes=16 * MIB),
    )(x)


def ring_sum_kernel(n, n_r, pa_ref, pb_ref, gd_ref, gu_ref, o_ref, od_ref, ou_ref, first_r, first_l,
                    second_out_r, second_out_l, second_r, second_l,
                    send_r, send_l, recv_r, recv_l, send_sem, recv_sem,
                    gsend_f, gsend_b, grecv_f, grecv_b, gsend_sem, grecv_sem):
    pos, rep_at = rep_ring(n_r)
    ahead, behind = rep_at(pos + 1), rep_at(pos - 1)
    me, right, left = enter(n, [("rep", ahead), ("rep", behind)])
    block = od_ref.shape[0]
    grads = (gd_ref, gu_ref)
    gsends = (gsend_f, gsend_b)
    grecvs = (grecv_f, grecv_b)

    def grad_rows(stream, step):
        dest = pos - 1 - step if stream == 0 else pos + 1 + step
        return pl.ds(pl.multiple_of(rep_at(dest) * block, block), block)

    def grad_hop(stream, step):
        if step == 0:
            src = grads[stream].at[grad_rows(stream, 0)]
        else:
            src = gsends[stream].at[step]
        return pltpu.make_async_remote_copy(
            src_ref=src, dst_ref=grecvs[stream].at[step],
            send_sem=gsend_sem.at[stream, step], recv_sem=grecv_sem.at[stream, step],
            device_id={"rep": ahead if stream == 0 else behind}, device_id_type=MESH_IDS)

    grad_copies = []
    grad_last = {}

    def grad_step(step):
        for stream in range(2):
            if step > 0:
                grad_last[stream].wait_recv()
                gsends[stream][step] = grecvs[stream][step - 1] + grads[stream][grad_rows(stream, step)]
            grad_last[stream] = grad_hop(stream, step)
            grad_last[stream].start()
            grad_copies.append(grad_last[stream])

    half = pa_ref.shape[1] // PARTS
    parts = (pa_ref, pb_ref)
    sends = (send_r, send_l)
    recvs = (recv_r, recv_l)

    def chunk_for(stream, step):
        if stream == 0:
            return lax.rem(me + 2 * n - 1 - step, n)
        return lax.rem(me + 1 + step, n)

    firsts = (first_r, first_l)
    second_outs = (second_out_r, second_out_l)
    seconds = (second_r, second_l)

    def hop(stream, part, step):
        rows = pl.ds(part * half, half)
        if step == 0:
            src = parts[stream].at[chunk_for(stream, 0), rows]
            dst = firsts[stream].at[rows]
        elif step == 1:
            src, dst = second_outs[stream].at[rows], seconds[stream].at[rows]
        else:
            src, dst = sends[stream].at[step, rows], recvs[stream].at[step, rows]
        return pltpu.make_async_remote_copy(
            src_ref=src, dst_ref=dst,
            send_sem=send_sem.at[stream, part, step], recv_sem=recv_sem.at[stream, part, step],
            device_id={"lz": right if stream == 0 else left}, device_id_type=MESH_IDS)

    order = [(stream, part) for part in range(PARTS) for stream in range(2)]
    copies = []
    last = {}
    for stream, part in order:
        last[stream, part] = hop(stream, part, 0)
        last[stream, part].start()
        copies.append(last[stream, part])
    grad_step(0)
    for step in range(1, max(n, n_r) - 1):
        if step < n_r - 1:
            grad_step(step)
        if step >= n - 1:
            continue
        for stream, part in order:
            rows = pl.ds(part * half, half)
            last[stream, part].wait_recv()
            here = parts[stream][chunk_for(stream, step), rows].astype(jnp.float32)
            if step == 1:
                second_outs[stream][rows] = (
                    firsts[stream][rows].astype(jnp.float32) + here).astype(second_outs[stream].dtype)
            elif step == 2:
                sends[stream][step, rows] = seconds[stream][rows].astype(jnp.float32) + here
            else:
                sends[stream][step, rows] = recvs[stream][step - 1, rows] + here
            last[stream, part] = hop(stream, part, step)
            last[stream, part].start()
            copies.append(last[stream, part])
    for stream, part in order:
        rows = pl.ds(part * half, half)
        last[stream, part].wait_recv()
        o_ref[stream, rows] = (
            recvs[stream][n - 2, rows] + parts[stream][me, rows].astype(jnp.float32)
        ).astype(o_ref.dtype)
    own = pl.ds(pl.multiple_of(rep_at(pos) * block, block), block)
    for stream, out in ((0, od_ref), (1, ou_ref)):
        grad_last[stream].wait_recv()
        out[...] = grecvs[stream][n_r - 2] + grads[stream][own]
    for copy in copies + grad_copies:
        copy.wait_send()


def ring_sum(first, second, grad_d, grad_u, n, n_r):
    _, rows, width = first.shape
    d_rows, d_cols = grad_d.shape
    block = d_rows // n_r
    return pl.pallas_call(
        functools.partial(ring_sum_kernel, n, n_r),
        out_shape=(
            jax.ShapeDtypeStruct((2, rows, width), first.dtype),
            jax.ShapeDtypeStruct((block, d_cols), grad_d.dtype),
            jax.ShapeDtypeStruct((block, d_cols), grad_u.dtype),
        ),
        in_specs=[pl.BlockSpec(memory_space=pltpu.VMEM)] * 4,
        out_specs=[pl.BlockSpec(memory_space=pltpu.VMEM)] * 3,
        scratch_shapes=[pltpu.VMEM((rows, width), first.dtype)] * 6
        + [pltpu.VMEM((n - 1, rows, width), jnp.float32)] * 4
        + [pltpu.SemaphoreType.DMA((2, PARTS, n - 1)), pltpu.SemaphoreType.DMA((2, PARTS, n - 1))]
        + [pltpu.VMEM((n_r - 1, block, d_cols), jnp.float32)] * 4
        + [pltpu.SemaphoreType.DMA((2, n_r - 1)), pltpu.SemaphoreType.DMA((2, n_r - 1))],
        compiler_params=pltpu.CompilerParams(
            collective_id=1, has_side_effects=True, vmem_limit_bytes=44 * MIB),
    )(first, second, grad_d, grad_u)


def y_exchange_kernel(n_y, x_ref, o_ref, send_sem, recv_sem):
    me = lax.axis_index("ly")
    barrier = pltpu.get_barrier_semaphore()
    for k in range(1, n_y):
        pl.semaphore_signal(
            barrier, inc=1, device_id={"ly": lax.rem(me + k, n_y)}, device_id_type=MESH_IDS)
    pl.semaphore_wait(barrier, n_y - 1)

    def exchange(k, src, dst):
        return pltpu.make_async_remote_copy(
            src_ref=src, dst_ref=dst, send_sem=send_sem.at[k], recv_sem=recv_sem.at[k],
            device_id={"ly": lax.rem(me + k, n_y)}, device_id_type=MESH_IDS)

    copies = []
    for k in range(1, n_y):
        copy = exchange(k, x_ref.at[:, lax.rem(me + k, n_y)], o_ref.at[:, me])
        copy.start()
        copies.append(copy)
    o_ref[:, me] = x_ref[:, me]
    for k in range(1, n_y):
        exchange(k, x_ref.at[:, me], o_ref.at[:, lax.rem(me + n_y - k, n_y)]).wait_recv()
    for copy in copies:
        copy.wait_send()


def y_exchange(x, call_id):
    n_y = x.shape[1]
    return pl.pallas_call(
        functools.partial(y_exchange_kernel, n_y),
        out_shape=jax.ShapeDtypeStruct(x.shape, x.dtype),
        in_specs=[pl.BlockSpec(memory_space=pltpu.VMEM)],
        out_specs=pl.BlockSpec(memory_space=pltpu.VMEM),
        scratch_shapes=[pltpu.SemaphoreType.DMA((n_y,)), pltpu.SemaphoreType.DMA((n_y,))],
        compiler_params=pltpu.CompilerParams(
            collective_id=call_id, has_side_effects=True, vmem_limit_bytes=8 * MIB),
    )(x)


def per_device(tokens, grad_out, lang_ids, slot_ids, w_up, w_down_t):
    feature_width = tokens.shape[1]
    capacity = CAPACITY
    keep_mask = slot_ids < capacity
    target = jnp.where(keep_mask, lang_ids * capacity + slot_ids, MODULES * capacity)
    safe_slot = jnp.minimum(slot_ids, capacity - 1)
    token_scale = 1.0 / TOK_DEV

    def place(values):
        buffer = (
            jnp.zeros((MODULES * capacity, feature_width), values.dtype)
            .at[target]
            .set(values, mode="drop")
        )
        return buffer.reshape(MODULES, capacity, feature_width)

    n_z = lax.axis_size("lz")

    def dispatch(first, second):
        both = jnp.stack([place(first), place(second)])
        lanes = 128
        by_y = y_exchange(both.reshape(2, MODULES, -1, lanes), 2)
        every = ring_gather(by_y.reshape(2, -1, feature_width), n_z)
        every = every.reshape(2, -1, feature_width)
        return every[0], every[1]

    def give_back(first, second, grad_d, grad_u):
        summed, grad_d, grad_u = ring_sum(
            first.reshape(n_z, -1, feature_width), second.reshape(n_z, -1, feature_width),
            grad_d, grad_u, n_z, lax.axis_size("rep"))
        summed = summed.reshape(2, -1, capacity, feature_width)
        back = y_exchange(summed.reshape(2, MODULES, -1, 128), 3)
        back = back.reshape(2, MODULES, capacity, feature_width)
        return back[0], back[1], grad_d, grad_u

    def collect(returned):
        picked = returned[lang_ids, safe_slot]
        return jnp.where(keep_mask[:, None], picked, jnp.zeros_like(picked))

    flat_tokens, flat_grads = dispatch(tokens, grad_out)
    pre_flat = jnp.dot(flat_tokens, w_up, preferred_element_type=jnp.float32)
    hidden_flat = gelu_value(pre_flat).astype(jnp.bfloat16)
    partial_rows = lax.dot_general(
        hidden_flat, w_down_t, (((1,), (1,)), ((), ())), preferred_element_type=jnp.float32
    ).astype(jnp.bfloat16)
    grad_down = lax.dot_general(
        flat_grads, hidden_flat, (((0,), (0,)), ((), ())), preferred_element_type=jnp.float32
    ) * token_scale
    d_hidden = jnp.dot(flat_grads, w_down_t, preferred_element_type=jnp.float32)
    d_pre = (d_hidden * gelu_slope(pre_flat)).astype(jnp.bfloat16)
    grad_up = lax.dot_general(
        flat_tokens, d_pre, (((0,), (0,)), ((), ())), preferred_element_type=jnp.float32
    ) * token_scale
    dx_part = lax.dot_general(
        d_pre, w_up, (((1,), (1,)), ((), ())), preferred_element_type=jnp.float32
    ).astype(jnp.bfloat16)
    returned, dx_back, grad_down, grad_up = give_back(partial_rows, dx_part, grad_down, grad_up)
    return (collect(returned), collect(dx_back), grad_up, grad_down)


def solution(mesh):
    n_lang = mesh.shape["lang"]
    groups = n_lang // MODULES
    devices = mesh.devices.reshape(MODULES, groups, mesh.shape["rep"])
    split_mesh = Mesh(devices, ("ly", "lz", "rep"))
    rows = P(("ly", "lz", "rep"), None)
    ids = P(("ly", "lz", "rep"))
    cols = P(None, ("ly", "lz"))
    return jax.shard_map(
        per_device,
        mesh=split_mesh,
        in_specs=(rows, rows, ids, ids, cols, cols),
        out_specs=(rows, rows, P("rep", ("ly", "lz")), P("rep", ("ly", "lz"))),
        check_vma=False,
    )
```

```python
import functools

import jax
import jax.numpy as jnp
from jax import lax
from jax.experimental import pallas as pl
from jax.experimental.pallas import tpu as pltpu
from jax.sharding import Mesh
from jax.sharding import PartitionSpec as P

MODULES = 8
TOK_DEV = 128
CAPACITY = 18


INV_ROOT_TWO = 0.7071067811865476
INV_ROOT_TAU = 0.3989422804014327


def gelu_value(values):
    return 0.5 * values * (1.0 + lax.erf(values * INV_ROOT_TWO))


def gelu_slope(values):
    return (
        0.5 * (1.0 + lax.erf(values * INV_ROOT_TWO))
        + values * jnp.exp(-0.5 * values * values) * INV_ROOT_TAU
    )

MESH_IDS = pl.DeviceIdType.MESH
MIB = 1024 * 1024
PARTS = 3


def enter(n, others=()):
    me = lax.axis_index("lz")
    right, left = lax.rem(me + 1, n), lax.rem(me + n - 1, n)
    peers = [("lz", left), ("lz", right)] + list(others)
    barrier = pltpu.get_barrier_semaphore()
    for axis, neighbour in peers:
        pl.semaphore_signal(barrier, inc=1, device_id={axis: neighbour}, device_id_type=MESH_IDS)
    pl.semaphore_wait(barrier, len(peers))
    return me, right, left


def rep_ring(n_r):
    rep = lax.axis_index("rep")
    chips = n_r // 2
    x, core = rep // 2, lax.rem(rep, 2)
    pos = core * (x + 1) + (1 - core) * lax.rem(n_r - x, n_r)

    def rep_at(p):
        p = lax.rem(p + 2 * n_r, n_r)
        up = 1 - lax.rem(p + n_r - 1, n_r) // chips
        return 2 * (up * (p - 1) + (1 - up) * lax.rem(n_r - p, n_r)) + up

    return pos, rep_at


def ring_gather_kernel(n, x_ref, o_ref, send_sem, recv_sem):
    me, right, left = enter(n)
    half = x_ref.shape[1] // PARTS
    o_ref[0, me] = x_ref[0]
    o_ref[1, me] = x_ref[1]

    def hop(stream, part, step):
        rows = pl.ds(part * half, half)
        if stream == 0:
            slot, peer = lax.rem(me - step + n, n), right
        else:
            slot, peer = lax.rem(me + step, n), left
        src = x_ref.at[stream, rows] if step == 0 else o_ref.at[stream, slot, rows]
        return pltpu.make_async_remote_copy(
            src_ref=src, dst_ref=o_ref.at[stream, slot, rows],
            send_sem=send_sem.at[stream, part, step], recv_sem=recv_sem.at[stream, part, step],
            device_id={"lz": peer}, device_id_type=MESH_IDS)

    order = [(stream, part) for part in range(PARTS) for stream in range(2)]
    copies = []
    last = {}
    for key in order:
        last[key] = hop(*key, 0)
        last[key].start()
        copies.append(last[key])
    for step in range(1, n - 1):
        for key in order:
            last[key].wait_recv()
            last[key] = hop(*key, step)
            last[key].start()
            copies.append(last[key])
    for key in order:
        last[key].wait_recv()
    for copy in copies:
        copy.wait_send()


def ring_gather(x, n):
    two, rows, width = x.shape
    return pl.pallas_call(
        functools.partial(ring_gather_kernel, n),
        out_shape=jax.ShapeDtypeStruct((two, n, rows, width), x.dtype),
        in_specs=[pl.BlockSpec(memory_space=pltpu.VMEM)],
        out_specs=pl.BlockSpec(memory_space=pltpu.VMEM),
        scratch_shapes=[pltpu.SemaphoreType.DMA((2, PARTS, n - 1)), pltpu.SemaphoreType.DMA((2, PARTS, n - 1))],
        compiler_params=pltpu.CompilerParams(
            collective_id=0, has_side_effects=True, vmem_limit_bytes=16 * MIB),
    )(x)


def ring_sum_kernel(n, n_r, pa_ref, pb_ref, gd_ref, gu_ref, o_ref, od_ref, ou_ref, first_r, first_l,
                    second_out_r, second_out_l, second_r, second_l,
                    send_r, send_l, recv_r, recv_l, send_sem, recv_sem,
                    gsend_f, gsend_b, grecv_f, grecv_b, gsend_sem, grecv_sem):
    pos, rep_at = rep_ring(n_r)
    ahead, behind = rep_at(pos + 1), rep_at(pos - 1)
    me, right, left = enter(n, [("rep", ahead), ("rep", behind)])
    block = od_ref.shape[0]
    grads = (gd_ref, gu_ref)
    gsends = (gsend_f, gsend_b)
    grecvs = (grecv_f, grecv_b)

    def grad_rows(stream, step):
        dest = pos - 1 - step if stream == 0 else pos + 1 + step
        return pl.ds(pl.multiple_of(rep_at(dest) * block, block), block)

    def grad_hop(stream, step):
        if step == 0:
            src = grads[stream].at[grad_rows(stream, 0)]
        else:
            src = gsends[stream].at[step]
        return pltpu.make_async_remote_copy(
            src_ref=src, dst_ref=grecvs[stream].at[step],
            send_sem=gsend_sem.at[stream, step], recv_sem=grecv_sem.at[stream, step],
            device_id={"rep": ahead if stream == 0 else behind}, device_id_type=MESH_IDS)

    grad_copies = []
    grad_last = {}

    def grad_step(step):
        for stream in range(2):
            if step > 0:
                grad_last[stream].wait_recv()
                gsends[stream][step] = grecvs[stream][step - 1] + grads[stream][grad_rows(stream, step)]
            grad_last[stream] = grad_hop(stream, step)
            grad_last[stream].start()
            grad_copies.append(grad_last[stream])

    half = pa_ref.shape[1] // PARTS
    parts = (pa_ref, pb_ref)
    sends = (send_r, send_l)
    recvs = (recv_r, recv_l)

    def chunk_for(stream, step):
        if stream == 0:
            return lax.rem(me + 2 * n - 1 - step, n)
        return lax.rem(me + 1 + step, n)

    firsts = (first_r, first_l)
    second_outs = (second_out_r, second_out_l)
    seconds = (second_r, second_l)

    def hop(stream, part, step):
        rows = pl.ds(part * half, half)
        if step == 0:
            src = parts[stream].at[chunk_for(stream, 0), rows]
            dst = firsts[stream].at[rows]
        elif step == 1:
            src, dst = second_outs[stream].at[rows], seconds[stream].at[rows]
        else:
            src, dst = sends[stream].at[step, rows], recvs[stream].at[step, rows]
        return pltpu.make_async_remote_copy(
            src_ref=src, dst_ref=dst,
            send_sem=send_sem.at[stream, part, step], recv_sem=recv_sem.at[stream, part, step],
            device_id={"lz": right if stream == 0 else left}, device_id_type=MESH_IDS)

    order = [(stream, part) for part in range(PARTS) for stream in range(2)]
    copies = []
    last = {}
    for stream, part in order:
        last[stream, part] = hop(stream, part, 0)
        last[stream, part].start()
        copies.append(last[stream, part])
    grad_step(0)
    for step in range(1, max(n, n_r) - 1):
        if step < n_r - 1:
            grad_step(step)
        if step >= n - 1:
            continue
        for stream, part in order:
            rows = pl.ds(part * half, half)
            last[stream, part].wait_recv()
            here = parts[stream][chunk_for(stream, step), rows].astype(jnp.float32)
            if step == 1:
                second_outs[stream][rows] = (
                    firsts[stream][rows].astype(jnp.float32) + here).astype(second_outs[stream].dtype)
            elif step == 2:
                sends[stream][step, rows] = seconds[stream][rows].astype(jnp.float32) + here
            else:
                sends[stream][step, rows] = recvs[stream][step - 1, rows] + here
            last[stream, part] = hop(stream, part, step)
            last[stream, part].start()
            copies.append(last[stream, part])
    for stream, part in order:
        rows = pl.ds(part * half, half)
        last[stream, part].wait_recv()
        o_ref[stream, rows] = (
            recvs[stream][n - 2, rows] + parts[stream][me, rows].astype(jnp.float32)
        ).astype(o_ref.dtype)
    own = pl.ds(pl.multiple_of(rep_at(pos) * block, block), block)
    for stream, out in ((0, od_ref), (1, ou_ref)):
        grad_last[stream].wait_recv()
        out[...] = grecvs[stream][n_r - 2] + grads[stream][own]
    for copy in copies + grad_copies:
        copy.wait_send()


def ring_sum(first, second, grad_d, grad_u, n, n_r):
    _, rows, width = first.shape
    d_rows, d_cols = grad_d.shape
    block = d_rows // n_r
    return pl.pallas_call(
        functools.partial(ring_sum_kernel, n, n_r),
        out_shape=(
            jax.ShapeDtypeStruct((2, rows, width), first.dtype),
            jax.ShapeDtypeStruct((block, d_cols), grad_d.dtype),
            jax.ShapeDtypeStruct((block, d_cols), grad_u.dtype),
        ),
        in_specs=[pl.BlockSpec(memory_space=pltpu.VMEM)] * 4,
        out_specs=[pl.BlockSpec(memory_space=pltpu.VMEM)] * 3,
        scratch_shapes=[pltpu.VMEM((rows, width), first.dtype)] * 6
        + [pltpu.VMEM((n - 1, rows, width), jnp.float32)] * 4
        + [pltpu.SemaphoreType.DMA((2, PARTS, n - 1)), pltpu.SemaphoreType.DMA((2, PARTS, n - 1))]
        + [pltpu.VMEM((n_r - 1, block, d_cols), jnp.float32)] * 4
        + [pltpu.SemaphoreType.DMA((2, n_r - 1)), pltpu.SemaphoreType.DMA((2, n_r - 1))],
        compiler_params=pltpu.CompilerParams(
            collective_id=1, has_side_effects=True, vmem_limit_bytes=44 * MIB),
    )(first, second, grad_d, grad_u)


def y_exchange_kernel(n_y, x_ref, o_ref, send_sem, recv_sem):
    me = lax.axis_index("ly")
    barrier = pltpu.get_barrier_semaphore()
    for k in range(1, n_y):
        pl.semaphore_signal(
            barrier, inc=1, device_id={"ly": lax.rem(me + k, n_y)}, device_id_type=MESH_IDS)
    pl.semaphore_wait(barrier, n_y - 1)

    def exchange(k, src, dst):
        return pltpu.make_async_remote_copy(
            src_ref=src, dst_ref=dst, send_sem=send_sem.at[k], recv_sem=recv_sem.at[k],
            device_id={"ly": lax.rem(me + k, n_y)}, device_id_type=MESH_IDS)

    copies = []
    for k in range(1, n_y):
        copy = exchange(k, x_ref.at[:, lax.rem(me + k, n_y)], o_ref.at[:, me])
        copy.start()
        copies.append(copy)
    o_ref[:, me] = x_ref[:, me]
    for k in range(1, n_y):
        exchange(k, x_ref.at[:, me], o_ref.at[:, lax.rem(me + n_y - k, n_y)]).wait_recv()
    for copy in copies:
        copy.wait_send()


def y_exchange(x, call_id):
    n_y = x.shape[1]
    return pl.pallas_call(
        functools.partial(y_exchange_kernel, n_y),
        out_shape=jax.ShapeDtypeStruct(x.shape, x.dtype),
        in_specs=[pl.BlockSpec(memory_space=pltpu.VMEM)],
        out_specs=pl.BlockSpec(memory_space=pltpu.VMEM),
        scratch_shapes=[pltpu.SemaphoreType.DMA((n_y,)), pltpu.SemaphoreType.DMA((n_y,))],
        compiler_params=pltpu.CompilerParams(
            collective_id=call_id, has_side_effects=True, vmem_limit_bytes=8 * MIB),
    )(x)


def per_device(tokens, grad_out, lang_ids, slot_ids, w_up, w_down_t):
    feature_width = tokens.shape[1]
    capacity = CAPACITY
    keep_mask = slot_ids < capacity
    target = jnp.where(keep_mask, lang_ids * capacity + slot_ids, MODULES * capacity)
    safe_slot = jnp.minimum(slot_ids, capacity - 1)
    token_scale = 1.0 / TOK_DEV

    def place(values):
        buffer = (
            jnp.zeros((2, MODULES * capacity, feature_width), values.dtype)
            .at[:, target]
            .set(values, mode="drop")
        )
        return buffer.reshape(2, MODULES, capacity, feature_width)

    n_z = lax.axis_size("lz")

    def dispatch(first, second):
        both = place(jnp.stack([first, second]))
        lanes = 128
        by_y = y_exchange(both.reshape(2, MODULES, -1, lanes), 2)
        every = ring_gather(by_y.reshape(2, -1, feature_width), n_z)
        every = every.reshape(2, -1, feature_width)
        return every[0], every[1]

    def give_back(first, second, grad_d, grad_u):
        summed, grad_d, grad_u = ring_sum(
            first.reshape(n_z, -1, feature_width), second.reshape(n_z, -1, feature_width),
            grad_d, grad_u, n_z, lax.axis_size("rep"))
        summed = summed.reshape(2, -1, capacity, feature_width)
        back = y_exchange(summed.reshape(2, MODULES, -1, 128), 3)
        back = back.reshape(2, MODULES, capacity, feature_width)
        return back, grad_d, grad_u

    def collect(returned):
        picked = returned[:, lang_ids, safe_slot]
        return jnp.where(keep_mask[None, :, None], picked, jnp.zeros_like(picked))

    flat_tokens, flat_grads = dispatch(tokens, grad_out)
    pre_flat = jnp.dot(flat_tokens, w_up, preferred_element_type=jnp.float32)
    hidden_flat = gelu_value(pre_flat).astype(jnp.bfloat16)
    partial_rows = lax.dot_general(
        hidden_flat, w_down_t, (((1,), (1,)), ((), ())), preferred_element_type=jnp.float32
    ).astype(jnp.bfloat16)
    grad_down = lax.dot_general(
        flat_grads, hidden_flat, (((0,), (0,)), ((), ())), preferred_element_type=jnp.float32
    ) * token_scale
    d_hidden = jnp.dot(flat_grads, w_down_t, preferred_element_type=jnp.float32)
    d_pre = (d_hidden * gelu_slope(pre_flat)).astype(jnp.bfloat16)
    grad_up = lax.dot_general(
        flat_tokens, d_pre, (((0,), (0,)), ((), ())), preferred_element_type=jnp.float32
    ) * token_scale
    dx_part = lax.dot_general(
        d_pre, w_up, (((1,), (1,)), ((), ())), preferred_element_type=jnp.float32
    ).astype(jnp.bfloat16)
    back, grad_down, grad_up = give_back(partial_rows, dx_part, grad_down, grad_up)
    picked = collect(back)
    return (picked[0], picked[1], grad_up, grad_down)


def solution(mesh):
    n_lang = mesh.shape["lang"]
    groups = n_lang // MODULES
    devices = mesh.devices.reshape(MODULES, groups, mesh.shape["rep"])
    split_mesh = Mesh(devices, ("ly", "lz", "rep"))
    rows = P(("ly", "lz", "rep"), None)
    ids = P(("ly", "lz", "rep"))
    cols = P(None, ("ly", "lz"))
    return jax.shard_map(
        per_device,
        mesh=split_mesh,
        in_specs=(rows, rows, ids, ids, cols, cols),
        out_specs=(rows, rows, P("rep", ("ly", "lz")), P("rep", ("ly", "lz"))),
        check_vma=False,
    )
```

```python
import functools

import jax
import jax.numpy as jnp
from jax import lax
from jax.experimental import pallas as pl
from jax.experimental.pallas import tpu as pltpu
from jax.sharding import Mesh
from jax.sharding import PartitionSpec as P

MODULES = 8
TOK_DEV = 128
CAPACITY = 18


INV_ROOT_TWO = 0.7071067811865476
INV_ROOT_TAU = 0.3989422804014327


def gelu_value(values):
    return 0.5 * values * (1.0 + lax.erf(values * INV_ROOT_TWO))


def gelu_slope(values):
    return (
        0.5 * (1.0 + lax.erf(values * INV_ROOT_TWO))
        + values * jnp.exp(-0.5 * values * values) * INV_ROOT_TAU
    )

MESH_IDS = pl.DeviceIdType.MESH
MIB = 1024 * 1024
PARTS = 3
WIDE_FROM = 3


def enter(n, others=()):
    me = lax.axis_index("lz")
    right, left = lax.rem(me + 1, n), lax.rem(me + n - 1, n)
    peers = [("lz", left), ("lz", right)] + list(others)
    barrier = pltpu.get_barrier_semaphore()
    for axis, neighbour in peers:
        pl.semaphore_signal(barrier, inc=1, device_id={axis: neighbour}, device_id_type=MESH_IDS)
    pl.semaphore_wait(barrier, len(peers))
    return me, right, left


def rep_ring(n_r):
    rep = lax.axis_index("rep")
    chips = n_r // 2
    x, core = rep // 2, lax.rem(rep, 2)
    pos = core * (x + 1) + (1 - core) * lax.rem(n_r - x, n_r)

    def rep_at(p):
        p = lax.rem(p + 2 * n_r, n_r)
        up = 1 - lax.rem(p + n_r - 1, n_r) // chips
        return 2 * (up * (p - 1) + (1 - up) * lax.rem(n_r - p, n_r)) + up

    return pos, rep_at


def ring_gather_kernel(n, x_ref, o_ref, send_sem, recv_sem):
    me, right, left = enter(n)
    half = x_ref.shape[1] // PARTS
    o_ref[0, me] = x_ref[0]
    o_ref[1, me] = x_ref[1]

    def hop(stream, part, step):
        rows = pl.ds(part * half, half)
        if stream == 0:
            slot, peer = lax.rem(me - step + n, n), right
        else:
            slot, peer = lax.rem(me + step, n), left
        src = x_ref.at[stream, rows] if step == 0 else o_ref.at[stream, slot, rows]
        return pltpu.make_async_remote_copy(
            src_ref=src, dst_ref=o_ref.at[stream, slot, rows],
            send_sem=send_sem.at[stream, part, step], recv_sem=recv_sem.at[stream, part, step],
            device_id={"lz": peer}, device_id_type=MESH_IDS)

    order = [(stream, part) for part in range(PARTS) for stream in range(2)]
    copies = []
    last = {}
    for key in order:
        last[key] = hop(*key, 0)
        last[key].start()
        copies.append(last[key])
    for step in range(1, n - 1):
        for key in order:
            last[key].wait_recv()
            last[key] = hop(*key, step)
            last[key].start()
            copies.append(last[key])
    for key in order:
        last[key].wait_recv()
    for copy in copies:
        copy.wait_send()


def ring_gather(x, n):
    two, rows, width = x.shape
    return pl.pallas_call(
        functools.partial(ring_gather_kernel, n),
        out_shape=jax.ShapeDtypeStruct((two, n, rows, width), x.dtype),
        in_specs=[pl.BlockSpec(memory_space=pltpu.VMEM)],
        out_specs=pl.BlockSpec(memory_space=pltpu.VMEM),
        scratch_shapes=[pltpu.SemaphoreType.DMA((2, PARTS, n - 1)), pltpu.SemaphoreType.DMA((2, PARTS, n - 1))],
        compiler_params=pltpu.CompilerParams(
            collective_id=0, has_side_effects=True, vmem_limit_bytes=16 * MIB),
    )(x)


def ring_sum_kernel(n, n_r, pa_ref, pb_ref, gd_ref, gu_ref, o_ref, od_ref, ou_ref, first_r, first_l,
                    second_out_r, second_out_l, second_r, second_l,
                    send_r, send_l, recv_r, recv_l, send_sem, recv_sem,
                    gsend_f, gsend_b, grecv_f, grecv_b, gsend_sem, grecv_sem):
    pos, rep_at = rep_ring(n_r)
    ahead, behind = rep_at(pos + 1), rep_at(pos - 1)
    me, right, left = enter(n, [("rep", ahead), ("rep", behind)])
    block = od_ref.shape[0]
    grads = (gd_ref, gu_ref)
    gsends = (gsend_f, gsend_b)
    grecvs = (grecv_f, grecv_b)

    def grad_rows(stream, step):
        dest = pos - 1 - step if stream == 0 else pos + 1 + step
        return pl.ds(pl.multiple_of(rep_at(dest) * block, block), block)

    def grad_hop(stream, step):
        if step == 0:
            src = grads[stream].at[grad_rows(stream, 0)]
        else:
            src = gsends[stream].at[step]
        return pltpu.make_async_remote_copy(
            src_ref=src, dst_ref=grecvs[stream].at[step],
            send_sem=gsend_sem.at[stream, step], recv_sem=grecv_sem.at[stream, step],
            device_id={"rep": ahead if stream == 0 else behind}, device_id_type=MESH_IDS)

    grad_copies = []
    grad_last = {}

    def grad_step(step):
        for stream in range(2):
            if step > 0:
                grad_last[stream].wait_recv()
                gsends[stream][step] = grecvs[stream][step - 1] + grads[stream][grad_rows(stream, step)]
            grad_last[stream] = grad_hop(stream, step)
            grad_last[stream].start()
            grad_copies.append(grad_last[stream])

    half = pa_ref.shape[1] // PARTS
    parts = (pa_ref, pb_ref)
    sends = (send_r, send_l)
    recvs = (recv_r, recv_l)

    def chunk_for(stream, step):
        if stream == 0:
            return lax.rem(me + 2 * n - 1 - step, n)
        return lax.rem(me + 1 + step, n)

    firsts = (first_r, first_l)
    second_outs = (second_out_r, second_out_l)
    seconds = (second_r, second_l)

    def hop(stream, part, step):
        rows = pl.ds(part * half, half)
        if step == 0:
            src = parts[stream].at[chunk_for(stream, 0), rows]
            dst = firsts[stream].at[rows]
        elif step < WIDE_FROM:
            src = second_outs[stream].at[step - 1, rows]
            dst = seconds[stream].at[step - 1, rows]
        else:
            src, dst = sends[stream].at[step, rows], recvs[stream].at[step, rows]
        return pltpu.make_async_remote_copy(
            src_ref=src, dst_ref=dst,
            send_sem=send_sem.at[stream, part, step], recv_sem=recv_sem.at[stream, part, step],
            device_id={"lz": right if stream == 0 else left}, device_id_type=MESH_IDS)

    order = [(stream, part) for part in range(PARTS) for stream in range(2)]
    copies = []
    last = {}
    for stream, part in order:
        last[stream, part] = hop(stream, part, 0)
        last[stream, part].start()
        copies.append(last[stream, part])
    grad_step(0)
    for step in range(1, max(n, n_r) - 1):
        if step < n_r - 1:
            grad_step(step)
        if step >= n - 1:
            continue
        for stream, part in order:
            rows = pl.ds(part * half, half)
            last[stream, part].wait_recv()
            here = parts[stream][chunk_for(stream, step), rows].astype(jnp.float32)
            if step == 1:
                came = firsts[stream][rows].astype(jnp.float32)
            elif step <= WIDE_FROM:
                came = seconds[stream][step - 2, rows].astype(jnp.float32)
            else:
                came = recvs[stream][step - 1, rows]
            if step < WIDE_FROM:
                second_outs[stream][step - 1, rows] = (came + here).astype(second_outs[stream].dtype)
            else:
                sends[stream][step, rows] = came + here
            last[stream, part] = hop(stream, part, step)
            last[stream, part].start()
            copies.append(last[stream, part])
    for stream, part in order:
        rows = pl.ds(part * half, half)
        last[stream, part].wait_recv()
        o_ref[stream, rows] = (
            recvs[stream][n - 2, rows] + parts[stream][me, rows].astype(jnp.float32)
        ).astype(o_ref.dtype)
    own = pl.ds(pl.multiple_of(rep_at(pos) * block, block), block)
    for stream, out in ((0, od_ref), (1, ou_ref)):
        grad_last[stream].wait_recv()
        out[...] = grecvs[stream][n_r - 2] + grads[stream][own]
    for copy in copies + grad_copies:
        copy.wait_send()


def ring_sum(first, second, grad_d, grad_u, n, n_r):
    _, rows, width = first.shape
    d_rows, d_cols = grad_d.shape
    block = d_rows // n_r
    return pl.pallas_call(
        functools.partial(ring_sum_kernel, n, n_r),
        out_shape=(
            jax.ShapeDtypeStruct((2, rows, width), first.dtype),
            jax.ShapeDtypeStruct((block, d_cols), grad_d.dtype),
            jax.ShapeDtypeStruct((block, d_cols), grad_u.dtype),
        ),
        in_specs=[pl.BlockSpec(memory_space=pltpu.VMEM)] * 4,
        out_specs=[pl.BlockSpec(memory_space=pltpu.VMEM)] * 3,
        scratch_shapes=[pltpu.VMEM((rows, width), first.dtype)] * 2
        + [pltpu.VMEM((WIDE_FROM - 1, rows, width), first.dtype)] * 4
        + [pltpu.VMEM((n - 1, rows, width), jnp.float32)] * 4
        + [pltpu.SemaphoreType.DMA((2, PARTS, n - 1)), pltpu.SemaphoreType.DMA((2, PARTS, n - 1))]
        + [pltpu.VMEM((n_r - 1, block, d_cols), jnp.float32)] * 4
        + [pltpu.SemaphoreType.DMA((2, n_r - 1)), pltpu.SemaphoreType.DMA((2, n_r - 1))],
        compiler_params=pltpu.CompilerParams(
            collective_id=1, has_side_effects=True, vmem_limit_bytes=44 * MIB),
    )(first, second, grad_d, grad_u)


def y_exchange_kernel(n_y, x_ref, o_ref, send_sem, recv_sem):
    me = lax.axis_index("ly")
    barrier = pltpu.get_barrier_semaphore()
    for k in range(1, n_y):
        pl.semaphore_signal(
            barrier, inc=1, device_id={"ly": lax.rem(me + k, n_y)}, device_id_type=MESH_IDS)
    pl.semaphore_wait(barrier, n_y - 1)

    def exchange(k, src, dst):
        return pltpu.make_async_remote_copy(
            src_ref=src, dst_ref=dst, send_sem=send_sem.at[k], recv_sem=recv_sem.at[k],
            device_id={"ly": lax.rem(me + k, n_y)}, device_id_type=MESH_IDS)

    copies = []
    for k in range(1, n_y):
        copy = exchange(k, x_ref.at[:, lax.rem(me + k, n_y)], o_ref.at[:, me])
        copy.start()
        copies.append(copy)
    o_ref[:, me] = x_ref[:, me]
    for k in range(1, n_y):
        exchange(k, x_ref.at[:, me], o_ref.at[:, lax.rem(me + n_y - k, n_y)]).wait_recv()
    for copy in copies:
        copy.wait_send()


def y_exchange(x, call_id):
    n_y = x.shape[1]
    return pl.pallas_call(
        functools.partial(y_exchange_kernel, n_y),
        out_shape=jax.ShapeDtypeStruct(x.shape, x.dtype),
        in_specs=[pl.BlockSpec(memory_space=pltpu.VMEM)],
        out_specs=pl.BlockSpec(memory_space=pltpu.VMEM),
        scratch_shapes=[pltpu.SemaphoreType.DMA((n_y,)), pltpu.SemaphoreType.DMA((n_y,))],
        compiler_params=pltpu.CompilerParams(
            collective_id=call_id, has_side_effects=True, vmem_limit_bytes=8 * MIB),
    )(x)


def per_device(tokens, grad_out, lang_ids, slot_ids, w_up, w_down_t):
    feature_width = tokens.shape[1]
    capacity = CAPACITY
    keep_mask = slot_ids < capacity
    target = jnp.where(keep_mask, lang_ids * capacity + slot_ids, MODULES * capacity)
    safe_slot = jnp.minimum(slot_ids, capacity - 1)
    token_scale = 1.0 / TOK_DEV

    def place(values):
        buffer = (
            jnp.zeros((MODULES * capacity, feature_width), values.dtype)
            .at[target]
            .set(values, mode="drop")
        )
        return buffer.reshape(MODULES, capacity, feature_width)

    n_z = lax.axis_size("lz")

    def dispatch(first, second):
        both = jnp.stack([place(first), place(second)])
        lanes = 128
        by_y = y_exchange(both.reshape(2, MODULES, -1, lanes), 2)
        every = ring_gather(by_y.reshape(2, -1, feature_width), n_z)
        every = every.reshape(2, -1, feature_width)
        return every[0], every[1]

    def give_back(first, second, grad_d, grad_u):
        summed, grad_d, grad_u = ring_sum(
            first.reshape(n_z, -1, feature_width), second.reshape(n_z, -1, feature_width),
            grad_d, grad_u, n_z, lax.axis_size("rep"))
        summed = summed.reshape(2, -1, capacity, feature_width)
        back = y_exchange(summed.reshape(2, MODULES, -1, 128), 3)
        back = back.reshape(2, MODULES, capacity, feature_width)
        return back[0], back[1], grad_d, grad_u

    def collect(returned):
        picked = returned[lang_ids, safe_slot]
        return jnp.where(keep_mask[:, None], picked, jnp.zeros_like(picked))

    flat_tokens, flat_grads = dispatch(tokens, grad_out)
    pre_flat = jnp.dot(flat_tokens, w_up, preferred_element_type=jnp.float32)
    hidden_flat = gelu_value(pre_flat).astype(jnp.bfloat16)
    partial_rows = lax.dot_general(
        hidden_flat, w_down_t, (((1,), (1,)), ((), ())), preferred_element_type=jnp.float32
    ).astype(jnp.bfloat16)
    grad_down = lax.dot_general(
        flat_grads, hidden_flat, (((0,), (0,)), ((), ())), preferred_element_type=jnp.float32
    ) * token_scale
    d_hidden = jnp.dot(flat_grads, w_down_t, preferred_element_type=jnp.float32)
    d_pre = (d_hidden * gelu_slope(pre_flat)).astype(jnp.bfloat16)
    grad_up = lax.dot_general(
        flat_tokens, d_pre, (((0,), (0,)), ((), ())), preferred_element_type=jnp.float32
    ) * token_scale
    dx_part = lax.dot_general(
        d_pre, w_up, (((1,), (1,)), ((), ())), preferred_element_type=jnp.float32
    ).astype(jnp.bfloat16)
    returned, dx_back, grad_down, grad_up = give_back(partial_rows, dx_part, grad_down, grad_up)
    return (collect(returned), collect(dx_back), grad_up, grad_down)


def solution(mesh):
    n_lang = mesh.shape["lang"]
    groups = n_lang // MODULES
    devices = mesh.devices.reshape(MODULES, groups, mesh.shape["rep"])
    split_mesh = Mesh(devices, ("ly", "lz", "rep"))
    rows = P(("ly", "lz", "rep"), None)
    ids = P(("ly", "lz", "rep"))
    cols = P(None, ("ly", "lz"))
    return jax.shard_map(
        per_device,
        mesh=split_mesh,
        in_specs=(rows, rows, ids, ids, cols, cols),
        out_specs=(rows, rows, P("rep", ("ly", "lz")), P("rep", ("ly", "lz"))),
        check_vma=False,
    )
```

```python
import functools

import jax
import jax.numpy as jnp
from jax import lax
from jax.experimental import pallas as pl
from jax.experimental.pallas import tpu as pltpu
from jax.sharding import Mesh
from jax.sharding import PartitionSpec as P

MODULES = 8
TOK_DEV = 128
CAPACITY = 18


INV_ROOT_TWO = 0.7071067811865476
INV_ROOT_TAU = 0.3989422804014327


def gelu_value(values):
    return 0.5 * values * (1.0 + lax.erf(values * INV_ROOT_TWO))


def gelu_slope(values):
    return (
        0.5 * (1.0 + lax.erf(values * INV_ROOT_TWO))
        + values * jnp.exp(-0.5 * values * values) * INV_ROOT_TAU
    )

MESH_IDS = pl.DeviceIdType.MESH
MIB = 1024 * 1024
PARTS = 3
WIDE_FROM = 3


def enter(n, others=()):
    me = lax.axis_index("lz")
    right, left = lax.rem(me + 1, n), lax.rem(me + n - 1, n)
    peers = [("lz", left), ("lz", right)] + list(others)
    barrier = pltpu.get_barrier_semaphore()
    for axis, neighbour in peers:
        pl.semaphore_signal(barrier, inc=1, device_id={axis: neighbour}, device_id_type=MESH_IDS)
    pl.semaphore_wait(barrier, len(peers))
    return me, right, left


def rep_ring(n_r):
    rep = lax.axis_index("rep")
    chips = n_r // 2
    x, core = rep // 2, lax.rem(rep, 2)
    pos = core * (x + 1) + (1 - core) * lax.rem(n_r - x, n_r)

    def rep_at(p):
        p = lax.rem(p + 2 * n_r, n_r)
        up = 1 - lax.rem(p + n_r - 1, n_r) // chips
        return 2 * (up * (p - 1) + (1 - up) * lax.rem(n_r - p, n_r)) + up

    return pos, rep_at


def ring_gather_kernel(n, x_ref, o_ref, send_sem, recv_sem, y_send, y_recv):
    n_y = x_ref.shape[1]
    me_y = lax.axis_index("ly")
    ys = [("ly", lax.rem(me_y + k, n_y)) for k in range(1, n_y)]
    me, right, left = enter(n, ys)

    def y_hop(k, src, dst):
        return pltpu.make_async_remote_copy(
            src_ref=src, dst_ref=dst, send_sem=y_send.at[k], recv_sem=y_recv.at[k],
            device_id={"ly": lax.rem(me_y + k, n_y)}, device_id_type=MESH_IDS)

    y_copies = []
    for k in range(1, n_y):
        copy = y_hop(k, x_ref.at[:, lax.rem(me_y + k, n_y)], o_ref.at[:, me, me_y])
        copy.start()
        y_copies.append(copy)
    o_ref[:, me, me_y] = x_ref[:, me_y]

    def hop(stream, k, step):
        source = lax.rem(me_y + n_y - k, n_y)
        if stream == 0:
            slot, peer = lax.rem(me - step + n, n), right
        else:
            slot, peer = lax.rem(me + step, n), left
        return pltpu.make_async_remote_copy(
            src_ref=o_ref.at[stream, slot, source], dst_ref=o_ref.at[stream, slot, source],
            send_sem=send_sem.at[stream, k, step], recv_sem=recv_sem.at[stream, k, step],
            device_id={"lz": peer}, device_id_type=MESH_IDS)

    copies = []
    last = {}
    for k in range(n_y):
        if k > 0:
            y_hop(k, x_ref.at[:, me_y], o_ref.at[:, me, lax.rem(me_y + n_y - k, n_y)]).wait_recv()
        for stream in range(2):
            last[stream, k] = hop(stream, k, 0)
            last[stream, k].start()
            copies.append(last[stream, k])
    for step in range(1, n - 1):
        for k in range(n_y):
            for stream in range(2):
                last[stream, k].wait_recv()
                last[stream, k] = hop(stream, k, step)
                last[stream, k].start()
                copies.append(last[stream, k])
    for key in last:
        last[key].wait_recv()
    for copy in copies + y_copies:
        copy.wait_send()


def ring_gather(x, n):
    two, n_y, rows, lanes = x.shape
    return pl.pallas_call(
        functools.partial(ring_gather_kernel, n),
        out_shape=jax.ShapeDtypeStruct((two, n, n_y, rows, lanes), x.dtype),
        in_specs=[pl.BlockSpec(memory_space=pltpu.VMEM)],
        out_specs=pl.BlockSpec(memory_space=pltpu.VMEM),
        scratch_shapes=[pltpu.SemaphoreType.DMA((2, n_y, n - 1)), pltpu.SemaphoreType.DMA((2, n_y, n - 1)),
                        pltpu.SemaphoreType.DMA((n_y,)), pltpu.SemaphoreType.DMA((n_y,))],
        compiler_params=pltpu.CompilerParams(
            collective_id=0, has_side_effects=True, vmem_limit_bytes=16 * MIB),
    )(x)


def ring_sum_kernel(n, n_r, pa_ref, pb_ref, gd_ref, gu_ref, o_ref, od_ref, ou_ref, first_r, first_l,
                    second_out_r, second_out_l, second_r, second_l,
                    send_r, send_l, recv_r, recv_l, send_sem, recv_sem,
                    gsend_f, gsend_b, grecv_f, grecv_b, gsend_sem, grecv_sem):
    pos, rep_at = rep_ring(n_r)
    ahead, behind = rep_at(pos + 1), rep_at(pos - 1)
    me, right, left = enter(n, [("rep", ahead), ("rep", behind)])
    block = od_ref.shape[0]
    grads = (gd_ref, gu_ref)
    gsends = (gsend_f, gsend_b)
    grecvs = (grecv_f, grecv_b)

    def grad_rows(stream, step):
        dest = pos - 1 - step if stream == 0 else pos + 1 + step
        return pl.ds(pl.multiple_of(rep_at(dest) * block, block), block)

    def grad_hop(stream, step):
        if step == 0:
            src = grads[stream].at[grad_rows(stream, 0)]
        else:
            src = gsends[stream].at[step]
        return pltpu.make_async_remote_copy(
            src_ref=src, dst_ref=grecvs[stream].at[step],
            send_sem=gsend_sem.at[stream, step], recv_sem=grecv_sem.at[stream, step],
            device_id={"rep": ahead if stream == 0 else behind}, device_id_type=MESH_IDS)

    grad_copies = []
    grad_last = {}

    def grad_step(step):
        for stream in range(2):
            if step > 0:
                grad_last[stream].wait_recv()
                gsends[stream][step] = grecvs[stream][step - 1] + grads[stream][grad_rows(stream, step)]
            grad_last[stream] = grad_hop(stream, step)
            grad_last[stream].start()
            grad_copies.append(grad_last[stream])

    half = pa_ref.shape[1] // PARTS
    parts = (pa_ref, pb_ref)
    sends = (send_r, send_l)
    recvs = (recv_r, recv_l)

    def chunk_for(stream, step):
        if stream == 0:
            return lax.rem(me + 2 * n - 1 - step, n)
        return lax.rem(me + 1 + step, n)

    firsts = (first_r, first_l)
    second_outs = (second_out_r, second_out_l)
    seconds = (second_r, second_l)

    def hop(stream, part, step):
        rows = pl.ds(part * half, half)
        if step == 0:
            src = parts[stream].at[chunk_for(stream, 0), rows]
            dst = firsts[stream].at[rows]
        elif step < WIDE_FROM:
            src = second_outs[stream].at[step - 1, rows]
            dst = seconds[stream].at[step - 1, rows]
        else:
            src, dst = sends[stream].at[step, rows], recvs[stream].at[step, rows]
        return pltpu.make_async_remote_copy(
            src_ref=src, dst_ref=dst,
            send_sem=send_sem.at[stream, part, step], recv_sem=recv_sem.at[stream, part, step],
            device_id={"lz": right if stream == 0 else left}, device_id_type=MESH_IDS)

    order = [(stream, part) for part in range(PARTS) for stream in range(2)]
    copies = []
    last = {}
    for stream, part in order:
        last[stream, part] = hop(stream, part, 0)
        last[stream, part].start()
        copies.append(last[stream, part])
    grad_step(0)
    for step in range(1, max(n, n_r) - 1):
        if step < n_r - 1:
            grad_step(step)
        if step >= n - 1:
            continue
        for stream, part in order:
            rows = pl.ds(part * half, half)
            last[stream, part].wait_recv()
            here = parts[stream][chunk_for(stream, step), rows].astype(jnp.float32)
            if step == 1:
                came = firsts[stream][rows].astype(jnp.float32)
            elif step <= WIDE_FROM:
                came = seconds[stream][step - 2, rows].astype(jnp.float32)
            else:
                came = recvs[stream][step - 1, rows]
            if step < WIDE_FROM:
                second_outs[stream][step - 1, rows] = (came + here).astype(second_outs[stream].dtype)
            else:
                sends[stream][step, rows] = came + here
            last[stream, part] = hop(stream, part, step)
            last[stream, part].start()
            copies.append(last[stream, part])
    for stream, part in order:
        rows = pl.ds(part * half, half)
        last[stream, part].wait_recv()
        o_ref[stream, rows] = (
            recvs[stream][n - 2, rows] + parts[stream][me, rows].astype(jnp.float32)
        ).astype(o_ref.dtype)
    own = pl.ds(pl.multiple_of(rep_at(pos) * block, block), block)
    for stream, out in ((0, od_ref), (1, ou_ref)):
        grad_last[stream].wait_recv()
        out[...] = grecvs[stream][n_r - 2] + grads[stream][own]
    for copy in copies + grad_copies:
        copy.wait_send()


def ring_sum(first, second, grad_d, grad_u, n, n_r):
    _, rows, width = first.shape
    d_rows, d_cols = grad_d.shape
    block = d_rows // n_r
    return pl.pallas_call(
        functools.partial(ring_sum_kernel, n, n_r),
        out_shape=(
            jax.ShapeDtypeStruct((2, rows, width), first.dtype),
            jax.ShapeDtypeStruct((block, d_cols), grad_d.dtype),
            jax.ShapeDtypeStruct((block, d_cols), grad_u.dtype),
        ),
        in_specs=[pl.BlockSpec(memory_space=pltpu.VMEM)] * 4,
        out_specs=[pl.BlockSpec(memory_space=pltpu.VMEM)] * 3,
        scratch_shapes=[pltpu.VMEM((rows, width), first.dtype)] * 2
        + [pltpu.VMEM((WIDE_FROM - 1, rows, width), first.dtype)] * 4
        + [pltpu.VMEM((n - 1, rows, width), jnp.float32)] * 4
        + [pltpu.SemaphoreType.DMA((2, PARTS, n - 1)), pltpu.SemaphoreType.DMA((2, PARTS, n - 1))]
        + [pltpu.VMEM((n_r - 1, block, d_cols), jnp.float32)] * 4
        + [pltpu.SemaphoreType.DMA((2, n_r - 1)), pltpu.SemaphoreType.DMA((2, n_r - 1))],
        compiler_params=pltpu.CompilerParams(
            collective_id=1, has_side_effects=True, vmem_limit_bytes=44 * MIB),
    )(first, second, grad_d, grad_u)


def y_exchange_kernel(n_y, x_ref, o_ref, send_sem, recv_sem):
    me = lax.axis_index("ly")
    barrier = pltpu.get_barrier_semaphore()
    for k in range(1, n_y):
        pl.semaphore_signal(
            barrier, inc=1, device_id={"ly": lax.rem(me + k, n_y)}, device_id_type=MESH_IDS)
    pl.semaphore_wait(barrier, n_y - 1)

    def exchange(k, src, dst):
        return pltpu.make_async_remote_copy(
            src_ref=src, dst_ref=dst, send_sem=send_sem.at[k], recv_sem=recv_sem.at[k],
            device_id={"ly": lax.rem(me + k, n_y)}, device_id_type=MESH_IDS)

    copies = []
    for k in range(1, n_y):
        copy = exchange(k, x_ref.at[:, lax.rem(me + k, n_y)], o_ref.at[:, me])
        copy.start()
        copies.append(copy)
    o_ref[:, me] = x_ref[:, me]
    for k in range(1, n_y):
        exchange(k, x_ref.at[:, me], o_ref.at[:, lax.rem(me + n_y - k, n_y)]).wait_recv()
    for copy in copies:
        copy.wait_send()


def y_exchange(x, call_id):
    n_y = x.shape[1]
    return pl.pallas_call(
        functools.partial(y_exchange_kernel, n_y),
        out_shape=jax.ShapeDtypeStruct(x.shape, x.dtype),
        in_specs=[pl.BlockSpec(memory_space=pltpu.VMEM)],
        out_specs=pl.BlockSpec(memory_space=pltpu.VMEM),
        scratch_shapes=[pltpu.SemaphoreType.DMA((n_y,)), pltpu.SemaphoreType.DMA((n_y,))],
        compiler_params=pltpu.CompilerParams(
            collective_id=call_id, has_side_effects=True, vmem_limit_bytes=8 * MIB),
    )(x)


def per_device(tokens, grad_out, lang_ids, slot_ids, w_up, w_down_t):
    feature_width = tokens.shape[1]
    capacity = CAPACITY
    keep_mask = slot_ids < capacity
    target = jnp.where(keep_mask, lang_ids * capacity + slot_ids, MODULES * capacity)
    safe_slot = jnp.minimum(slot_ids, capacity - 1)
    token_scale = 1.0 / TOK_DEV

    def place(values):
        buffer = (
            jnp.zeros((MODULES * capacity, feature_width), values.dtype)
            .at[target]
            .set(values, mode="drop")
        )
        return buffer.reshape(MODULES, capacity, feature_width)

    n_z = lax.axis_size("lz")

    def dispatch(first, second):
        both = jnp.stack([place(first), place(second)])
        lanes = 128
        every = ring_gather(both.reshape(2, MODULES, -1, lanes), n_z)
        every = every.reshape(2, -1, feature_width)
        return every[0], every[1]

    def give_back(first, second, grad_d, grad_u):
        summed, grad_d, grad_u = ring_sum(
            first.reshape(n_z, -1, feature_width), second.reshape(n_z, -1, feature_width),
            grad_d, grad_u, n_z, lax.axis_size("rep"))
        summed = summed.reshape(2, -1, capacity, feature_width)
        back = y_exchange(summed.reshape(2, MODULES, -1, 128), 3)
        back = back.reshape(2, MODULES, capacity, feature_width)
        return back[0], back[1], grad_d, grad_u

    def collect(returned):
        picked = returned[lang_ids, safe_slot]
        return jnp.where(keep_mask[:, None], picked, jnp.zeros_like(picked))

    flat_tokens, flat_grads = dispatch(tokens, grad_out)
    pre_flat = jnp.dot(flat_tokens, w_up, preferred_element_type=jnp.float32)
    hidden_flat = gelu_value(pre_flat).astype(jnp.bfloat16)
    partial_rows = lax.dot_general(
        hidden_flat, w_down_t, (((1,), (1,)), ((), ())), preferred_element_type=jnp.float32
    ).astype(jnp.bfloat16)
    grad_down = lax.dot_general(
        flat_grads, hidden_flat, (((0,), (0,)), ((), ())), preferred_element_type=jnp.float32
    ) * token_scale
    d_hidden = jnp.dot(flat_grads, w_down_t, preferred_element_type=jnp.float32)
    d_pre = (d_hidden * gelu_slope(pre_flat)).astype(jnp.bfloat16)
    grad_up = lax.dot_general(
        flat_tokens, d_pre, (((0,), (0,)), ((), ())), preferred_element_type=jnp.float32
    ) * token_scale
    dx_part = lax.dot_general(
        d_pre, w_up, (((1,), (1,)), ((), ())), preferred_element_type=jnp.float32
    ).astype(jnp.bfloat16)
    returned, dx_back, grad_down, grad_up = give_back(partial_rows, dx_part, grad_down, grad_up)
    return (collect(returned), collect(dx_back), grad_up, grad_down)


def solution(mesh):
    n_lang = mesh.shape["lang"]
    groups = n_lang // MODULES
    devices = mesh.devices.reshape(MODULES, groups, mesh.shape["rep"])
    split_mesh = Mesh(devices, ("ly", "lz", "rep"))
    rows = P(("ly", "lz", "rep"), None)
    ids = P(("ly", "lz", "rep"))
    cols = P(None, ("ly", "lz"))
    return jax.shard_map(
        per_device,
        mesh=split_mesh,
        in_specs=(rows, rows, ids, ids, cols, cols),
        out_specs=(rows, rows, P("rep", ("ly", "lz")), P("rep", ("ly", "lz"))),
        check_vma=False,
    )
```

```python
import functools

import jax
import jax.numpy as jnp
from jax import lax
from jax.experimental import pallas as pl
from jax.experimental.pallas import tpu as pltpu
from jax.sharding import Mesh
from jax.sharding import PartitionSpec as P

MODULES = 8
TOK_DEV = 128
CAPACITY = 18


INV_ROOT_TWO = 0.7071067811865476
INV_ROOT_TAU = 0.3989422804014327


def gelu_value(values):
    return 0.5 * values * (1.0 + lax.erf(values * INV_ROOT_TWO))


def gelu_slope(values):
    return (
        0.5 * (1.0 + lax.erf(values * INV_ROOT_TWO))
        + values * jnp.exp(-0.5 * values * values) * INV_ROOT_TAU
    )

MESH_IDS = pl.DeviceIdType.MESH
MIB = 1024 * 1024
PARTS = 3
WIDE_FROM = 4


def enter(n, others=()):
    me = lax.axis_index("lz")
    right, left = lax.rem(me + 1, n), lax.rem(me + n - 1, n)
    peers = [("lz", left), ("lz", right)] + list(others)
    barrier = pltpu.get_barrier_semaphore()
    for axis, neighbour in peers:
        pl.semaphore_signal(barrier, inc=1, device_id={axis: neighbour}, device_id_type=MESH_IDS)
    pl.semaphore_wait(barrier, len(peers))
    return me, right, left


def rep_ring(n_r):
    rep = lax.axis_index("rep")
    chips = n_r // 2
    x, core = rep // 2, lax.rem(rep, 2)
    pos = core * (x + 1) + (1 - core) * lax.rem(n_r - x, n_r)

    def rep_at(p):
        p = lax.rem(p + 2 * n_r, n_r)
        up = 1 - lax.rem(p + n_r - 1, n_r) // chips
        return 2 * (up * (p - 1) + (1 - up) * lax.rem(n_r - p, n_r)) + up

    return pos, rep_at


def ring_gather_kernel(n, x_ref, o_ref, send_sem, recv_sem):
    me, right, left = enter(n)
    half = x_ref.shape[1] // PARTS
    o_ref[0, me] = x_ref[0]
    o_ref[1, me] = x_ref[1]

    def hop(stream, part, step):
        rows = pl.ds(part * half, half)
        if stream == 0:
            slot, peer = lax.rem(me - step + n, n), right
        else:
            slot, peer = lax.rem(me + step, n), left
        src = x_ref.at[stream, rows] if step == 0 else o_ref.at[stream, slot, rows]
        return pltpu.make_async_remote_copy(
            src_ref=src, dst_ref=o_ref.at[stream, slot, rows],
            send_sem=send_sem.at[stream, part, step], recv_sem=recv_sem.at[stream, part, step],
            device_id={"lz": peer}, device_id_type=MESH_IDS)

    order = [(stream, part) for part in range(PARTS) for stream in range(2)]
    copies = []
    last = {}
    for key in order:
        last[key] = hop(*key, 0)
        last[key].start()
        copies.append(last[key])
    for step in range(1, n - 1):
        for key in order:
            last[key].wait_recv()
            last[key] = hop(*key, step)
            last[key].start()
            copies.append(last[key])
    for key in order:
        last[key].wait_recv()
    for copy in copies:
        copy.wait_send()


def ring_gather(x, n):
    two, rows, width = x.shape
    return pl.pallas_call(
        functools.partial(ring_gather_kernel, n),
        out_shape=jax.ShapeDtypeStruct((two, n, rows, width), x.dtype),
        in_specs=[pl.BlockSpec(memory_space=pltpu.VMEM)],
        out_specs=pl.BlockSpec(memory_space=pltpu.VMEM),
        scratch_shapes=[pltpu.SemaphoreType.DMA((2, PARTS, n - 1)), pltpu.SemaphoreType.DMA((2, PARTS, n - 1))],
        compiler_params=pltpu.CompilerParams(
            collective_id=0, has_side_effects=True, vmem_limit_bytes=16 * MIB),
    )(x)


def ring_sum_kernel(n, n_r, pa_ref, pb_ref, gd_ref, gu_ref, o_ref, od_ref, ou_ref, first_r, first_l,
                    second_out_r, second_out_l, second_r, second_l,
                    send_r, send_l, recv_r, recv_l, send_sem, recv_sem,
                    gsend_f, gsend_b, grecv_f, grecv_b, gsend_sem, grecv_sem):
    pos, rep_at = rep_ring(n_r)
    ahead, behind = rep_at(pos + 1), rep_at(pos - 1)
    me, right, left = enter(n, [("rep", ahead), ("rep", behind)])
    block = od_ref.shape[0]
    grads = (gd_ref, gu_ref)
    gsends = (gsend_f, gsend_b)
    grecvs = (grecv_f, grecv_b)

    def grad_rows(stream, step):
        dest = pos - 1 - step if stream == 0 else pos + 1 + step
        return pl.ds(pl.multiple_of(rep_at(dest) * block, block), block)

    def grad_hop(stream, step):
        if step == 0:
            src = grads[stream].at[grad_rows(stream, 0)]
        else:
            src = gsends[stream].at[step]
        return pltpu.make_async_remote_copy(
            src_ref=src, dst_ref=grecvs[stream].at[step],
            send_sem=gsend_sem.at[stream, step], recv_sem=grecv_sem.at[stream, step],
            device_id={"rep": ahead if stream == 0 else behind}, device_id_type=MESH_IDS)

    grad_copies = []
    grad_last = {}

    def grad_step(step):
        for stream in range(2):
            if step > 0:
                grad_last[stream].wait_recv()
                gsends[stream][step] = grecvs[stream][step - 1] + grads[stream][grad_rows(stream, step)]
            grad_last[stream] = grad_hop(stream, step)
            grad_last[stream].start()
            grad_copies.append(grad_last[stream])

    half = pa_ref.shape[1] // PARTS
    parts = (pa_ref, pb_ref)
    sends = (send_r, send_l)
    recvs = (recv_r, recv_l)

    def chunk_for(stream, step):
        if stream == 0:
            return lax.rem(me + 2 * n - 1 - step, n)
        return lax.rem(me + 1 + step, n)

    firsts = (first_r, first_l)
    second_outs = (second_out_r, second_out_l)
    seconds = (second_r, second_l)

    def hop(stream, part, step):
        rows = pl.ds(part * half, half)
        if step == 0:
            src = parts[stream].at[chunk_for(stream, 0), rows]
            dst = firsts[stream].at[rows]
        elif step < WIDE_FROM:
            src = second_outs[stream].at[step - 1, rows]
            dst = seconds[stream].at[step - 1, rows]
        else:
            src, dst = sends[stream].at[step, rows], recvs[stream].at[step, rows]
        return pltpu.make_async_remote_copy(
            src_ref=src, dst_ref=dst,
            send_sem=send_sem.at[stream, part, step], recv_sem=recv_sem.at[stream, part, step],
            device_id={"lz": right if stream == 0 else left}, device_id_type=MESH_IDS)

    order = [(stream, part) for part in range(PARTS) for stream in range(2)]
    copies = []
    last = {}
    for stream, part in order:
        last[stream, part] = hop(stream, part, 0)
        last[stream, part].start()
        copies.append(last[stream, part])
    grad_step(0)
    for step in range(1, max(n, n_r) - 1):
        if step < n_r - 1:
            grad_step(step)
        if step >= n - 1:
            continue
        for stream, part in order:
            rows = pl.ds(part * half, half)
            last[stream, part].wait_recv()
            here = parts[stream][chunk_for(stream, step), rows].astype(jnp.float32)
            if step == 1:
                came = firsts[stream][rows].astype(jnp.float32)
            elif step <= WIDE_FROM:
                came = seconds[stream][step - 2, rows].astype(jnp.float32)
            else:
                came = recvs[stream][step - 1, rows]
            if step < WIDE_FROM:
                second_outs[stream][step - 1, rows] = (came + here).astype(second_outs[stream].dtype)
            else:
                sends[stream][step, rows] = came + here
            last[stream, part] = hop(stream, part, step)
            last[stream, part].start()
            copies.append(last[stream, part])
    for stream, part in order:
        rows = pl.ds(part * half, half)
        last[stream, part].wait_recv()
        o_ref[stream, rows] = (
            recvs[stream][n - 2, rows] + parts[stream][me, rows].astype(jnp.float32)
        ).astype(o_ref.dtype)
    own = pl.ds(pl.multiple_of(rep_at(pos) * block, block), block)
    for stream, out in ((0, od_ref), (1, ou_ref)):
        grad_last[stream].wait_recv()
        out[...] = grecvs[stream][n_r - 2] + grads[stream][own]
    for copy in copies + grad_copies:
        copy.wait_send()


def ring_sum(first, second, grad_d, grad_u, n, n_r):
    _, rows, width = first.shape
    d_rows, d_cols = grad_d.shape
    block = d_rows // n_r
    return pl.pallas_call(
        functools.partial(ring_sum_kernel, n, n_r),
        out_shape=(
            jax.ShapeDtypeStruct((2, rows, width), first.dtype),
            jax.ShapeDtypeStruct((block, d_cols), grad_d.dtype),
            jax.ShapeDtypeStruct((block, d_cols), grad_u.dtype),
        ),
        in_specs=[pl.BlockSpec(memory_space=pltpu.VMEM)] * 4,
        out_specs=[pl.BlockSpec(memory_space=pltpu.VMEM)] * 3,
        scratch_shapes=[pltpu.VMEM((rows, width), first.dtype)] * 2
        + [pltpu.VMEM((WIDE_FROM - 1, rows, width), first.dtype)] * 4
        + [pltpu.VMEM((n - 1, rows, width), jnp.float32)] * 4
        + [pltpu.SemaphoreType.DMA((2, PARTS, n - 1)), pltpu.SemaphoreType.DMA((2, PARTS, n - 1))]
        + [pltpu.VMEM((n_r - 1, block, d_cols), jnp.float32)] * 4
        + [pltpu.SemaphoreType.DMA((2, n_r - 1)), pltpu.SemaphoreType.DMA((2, n_r - 1))],
        compiler_params=pltpu.CompilerParams(
            collective_id=1, has_side_effects=True, vmem_limit_bytes=44 * MIB),
    )(first, second, grad_d, grad_u)


def y_exchange_kernel(n_y, x_ref, o_ref, send_sem, recv_sem):
    me = lax.axis_index("ly")
    barrier = pltpu.get_barrier_semaphore()
    for k in range(1, n_y):
        pl.semaphore_signal(
            barrier, inc=1, device_id={"ly": lax.rem(me + k, n_y)}, device_id_type=MESH_IDS)
    pl.semaphore_wait(barrier, n_y - 1)

    def exchange(k, src, dst):
        return pltpu.make_async_remote_copy(
            src_ref=src, dst_ref=dst, send_sem=send_sem.at[k], recv_sem=recv_sem.at[k],
            device_id={"ly": lax.rem(me + k, n_y)}, device_id_type=MESH_IDS)

    copies = []
    for k in range(1, n_y):
        copy = exchange(k, x_ref.at[:, lax.rem(me + k, n_y)], o_ref.at[:, me])
        copy.start()
        copies.append(copy)
    o_ref[:, me] = x_ref[:, me]
    for k in range(1, n_y):
        exchange(k, x_ref.at[:, me], o_ref.at[:, lax.rem(me + n_y - k, n_y)]).wait_recv()
    for copy in copies:
        copy.wait_send()


def y_exchange(x, call_id):
    n_y = x.shape[1]
    return pl.pallas_call(
        functools.partial(y_exchange_kernel, n_y),
        out_shape=jax.ShapeDtypeStruct(x.shape, x.dtype),
        in_specs=[pl.BlockSpec(memory_space=pltpu.VMEM)],
        out_specs=pl.BlockSpec(memory_space=pltpu.VMEM),
        scratch_shapes=[pltpu.SemaphoreType.DMA((n_y,)), pltpu.SemaphoreType.DMA((n_y,))],
        compiler_params=pltpu.CompilerParams(
            collective_id=call_id, has_side_effects=True, vmem_limit_bytes=8 * MIB),
    )(x)


def per_device(tokens, grad_out, lang_ids, slot_ids, w_up, w_down_t):
    feature_width = tokens.shape[1]
    capacity = CAPACITY
    keep_mask = slot_ids < capacity
    target = jnp.where(keep_mask, lang_ids * capacity + slot_ids, MODULES * capacity)
    safe_slot = jnp.minimum(slot_ids, capacity - 1)
    token_scale = 1.0 / TOK_DEV

    def place(values):
        buffer = (
            jnp.zeros((MODULES * capacity, feature_width), values.dtype)
            .at[target]
            .set(values, mode="drop")
        )
        return buffer.reshape(MODULES, capacity, feature_width)

    n_z = lax.axis_size("lz")

    def dispatch(first, second):
        both = jnp.stack([place(first), place(second)])
        lanes = 128
        by_y = y_exchange(both.reshape(2, MODULES, -1, lanes), 2)
        every = ring_gather(by_y.reshape(2, -1, feature_width), n_z)
        every = every.reshape(2, -1, feature_width)
        return every[0], every[1]

    def give_back(first, second, grad_d, grad_u):
        summed, grad_d, grad_u = ring_sum(
            first.reshape(n_z, -1, feature_width), second.reshape(n_z, -1, feature_width),
            grad_d, grad_u, n_z, lax.axis_size("rep"))
        summed = summed.reshape(2, -1, capacity, feature_width)
        back = y_exchange(summed.reshape(2, MODULES, -1, 128), 3)
        back = back.reshape(2, MODULES, capacity, feature_width)
        return back[0], back[1], grad_d, grad_u

    def collect(returned):
        picked = returned[lang_ids, safe_slot]
        return jnp.where(keep_mask[:, None], picked, jnp.zeros_like(picked))

    flat_tokens, flat_grads = dispatch(tokens, grad_out)
    pre_flat = jnp.dot(flat_tokens, w_up, preferred_element_type=jnp.float32)
    hidden_flat = gelu_value(pre_flat).astype(jnp.bfloat16)
    partial_rows = lax.dot_general(
        hidden_flat, w_down_t, (((1,), (1,)), ((), ())), preferred_element_type=jnp.float32
    ).astype(jnp.bfloat16)
    grad_down = lax.dot_general(
        flat_grads, hidden_flat, (((0,), (0,)), ((), ())), preferred_element_type=jnp.float32
    ) * token_scale
    d_hidden = jnp.dot(flat_grads, w_down_t, preferred_element_type=jnp.float32)
    d_pre = (d_hidden * gelu_slope(pre_flat)).astype(jnp.bfloat16)
    grad_up = lax.dot_general(
        flat_tokens, d_pre, (((0,), (0,)), ((), ())), preferred_element_type=jnp.float32
    ) * token_scale
    dx_part = lax.dot_general(
        d_pre, w_up, (((1,), (1,)), ((), ())), preferred_element_type=jnp.float32
    ).astype(jnp.bfloat16)
    returned, dx_back, grad_down, grad_up = give_back(partial_rows, dx_part, grad_down, grad_up)
    return (collect(returned), collect(dx_back), grad_up, grad_down)


def solution(mesh):
    n_lang = mesh.shape["lang"]
    groups = n_lang // MODULES
    devices = mesh.devices.reshape(MODULES, groups, mesh.shape["rep"])
    split_mesh = Mesh(devices, ("ly", "lz", "rep"))
    rows = P(("ly", "lz", "rep"), None)
    ids = P(("ly", "lz", "rep"))
    cols = P(None, ("ly", "lz"))
    return jax.shard_map(
        per_device,
        mesh=split_mesh,
        in_specs=(rows, rows, ids, ids, cols, cols),
        out_specs=(rows, rows, P("rep", ("ly", "lz")), P("rep", ("ly", "lz"))),
        check_vma=False,
    )
```

```python
import functools

import jax
import jax.numpy as jnp
from jax import lax
from jax.experimental import pallas as pl
from jax.experimental.pallas import tpu as pltpu
from jax.sharding import Mesh
from jax.sharding import PartitionSpec as P

MODULES = 8
TOK_DEV = 128
CAPACITY = 18


INV_ROOT_TWO = 0.7071067811865476
INV_ROOT_TAU = 0.3989422804014327


def gelu_value(values):
    return 0.5 * values * (1.0 + lax.erf(values * INV_ROOT_TWO))


def gelu_slope(values):
    return (
        0.5 * (1.0 + lax.erf(values * INV_ROOT_TWO))
        + values * jnp.exp(-0.5 * values * values) * INV_ROOT_TAU
    )

MESH_IDS = pl.DeviceIdType.MESH
MIB = 1024 * 1024
PARTS = 3
WIDE_FROM = 4


def enter(n, others=()):
    me = lax.axis_index("lz")
    right, left = lax.rem(me + 1, n), lax.rem(me + n - 1, n)
    peers = [("lz", left), ("lz", right)] + list(others)
    barrier = pltpu.get_barrier_semaphore()
    for axis, neighbour in peers:
        pl.semaphore_signal(barrier, inc=1, device_id={axis: neighbour}, device_id_type=MESH_IDS)
    pl.semaphore_wait(barrier, len(peers))
    return me, right, left


def rep_ring(n_r):
    rep = lax.axis_index("rep")
    chips = n_r // 2
    x, core = rep // 2, lax.rem(rep, 2)
    pos = core * (x + 1) + (1 - core) * lax.rem(n_r - x, n_r)

    def rep_at(p):
        p = lax.rem(p + 2 * n_r, n_r)
        up = 1 - lax.rem(p + n_r - 1, n_r) // chips
        return 2 * (up * (p - 1) + (1 - up) * lax.rem(n_r - p, n_r)) + up

    return pos, rep_at


def ring_gather_kernel(n, x_ref, o_ref, send_sem, recv_sem):
    me, right, left = enter(n)
    half = x_ref.shape[1] // PARTS
    o_ref[0, me] = x_ref[0]
    o_ref[1, me] = x_ref[1]

    def hop(stream, part, step):
        rows = pl.ds(part * half, half)
        if stream == 0:
            slot, peer = lax.rem(me - step + n, n), right
        else:
            slot, peer = lax.rem(me + step, n), left
        src = x_ref.at[stream, rows] if step == 0 else o_ref.at[stream, slot, rows]
        return pltpu.make_async_remote_copy(
            src_ref=src, dst_ref=o_ref.at[stream, slot, rows],
            send_sem=send_sem.at[stream, part, step], recv_sem=recv_sem.at[stream, part, step],
            device_id={"lz": peer}, device_id_type=MESH_IDS)

    order = [(stream, part) for part in range(PARTS) for stream in range(2)]
    copies = []
    last = {}
    for key in order:
        last[key] = hop(*key, 0)
        last[key].start()
        copies.append(last[key])
    for step in range(1, n - 1):
        for key in order:
            last[key].wait_recv()
            last[key] = hop(*key, step)
            last[key].start()
            copies.append(last[key])
    for key in order:
        last[key].wait_recv()
    for copy in copies:
        copy.wait_send()


def ring_gather(x, n):
    two, rows, width = x.shape
    return pl.pallas_call(
        functools.partial(ring_gather_kernel, n),
        out_shape=jax.ShapeDtypeStruct((two, n, rows, width), x.dtype),
        in_specs=[pl.BlockSpec(memory_space=pltpu.VMEM)],
        out_specs=pl.BlockSpec(memory_space=pltpu.VMEM),
        scratch_shapes=[pltpu.SemaphoreType.DMA((2, PARTS, n - 1)), pltpu.SemaphoreType.DMA((2, PARTS, n - 1))],
        compiler_params=pltpu.CompilerParams(
            collective_id=0, has_side_effects=True, vmem_limit_bytes=16 * MIB),
    )(x)


def ring_sum_kernel(n, n_r, pa_ref, pb_ref, gd_ref, gu_ref, o_ref, od_ref, ou_ref, first_r, first_l,
                    second_out_r, second_out_l, second_r, second_l,
                    send_r, send_l, recv_r, recv_l, send_sem, recv_sem,
                    gsend_f, gsend_b, grecv_f, grecv_b, gsend_sem, grecv_sem):
    pos, rep_at = rep_ring(n_r)
    ahead, behind = rep_at(pos + 1), rep_at(pos - 1)
    me, right, left = enter(n, [("rep", ahead), ("rep", behind)])
    block = od_ref.shape[0]
    grads = (gd_ref, gu_ref)
    gsends = (gsend_f, gsend_b)
    grecvs = (grecv_f, grecv_b)

    def grad_rows(stream, step):
        dest = pos - 1 - step if stream == 0 else pos + 1 + step
        return pl.ds(pl.multiple_of(rep_at(dest) * block, block), block)

    def grad_hop(stream, step):
        if step == 0:
            src = grads[stream].at[grad_rows(stream, 0)]
        else:
            src = gsends[stream].at[step]
        return pltpu.make_async_remote_copy(
            src_ref=src, dst_ref=grecvs[stream].at[step],
            send_sem=gsend_sem.at[stream, step], recv_sem=grecv_sem.at[stream, step],
            device_id={"rep": ahead if stream == 0 else behind}, device_id_type=MESH_IDS)

    grad_copies = []
    grad_last = {}

    def grad_step(step):
        for stream in range(2):
            if step > 0:
                grad_last[stream].wait_recv()
                gsends[stream][step] = grecvs[stream][step - 1] + grads[stream][grad_rows(stream, step)]
            grad_last[stream] = grad_hop(stream, step)
            grad_last[stream].start()
            grad_copies.append(grad_last[stream])

    half = pa_ref.shape[1] // PARTS
    parts = (pa_ref, pb_ref)
    sends = (send_r, send_l)
    recvs = (recv_r, recv_l)

    def chunk_for(stream, step):
        if stream == 0:
            return lax.rem(me + 2 * n - 1 - step, n)
        return lax.rem(me + 1 + step, n)

    firsts = (first_r, first_l)
    second_outs = (second_out_r, second_out_l)
    seconds = (second_r, second_l)

    def hop(stream, part, step):
        rows = pl.ds(part * half, half)
        if step == 0:
            src = parts[stream].at[chunk_for(stream, 0), rows]
            dst = firsts[stream].at[rows]
        elif step < WIDE_FROM:
            src = second_outs[stream].at[step - 1, rows]
            dst = seconds[stream].at[step - 1, rows]
        else:
            src, dst = sends[stream].at[step, rows], recvs[stream].at[step, rows]
        return pltpu.make_async_remote_copy(
            src_ref=src, dst_ref=dst,
            send_sem=send_sem.at[stream, part, step], recv_sem=recv_sem.at[stream, part, step],
            device_id={"lz": right if stream == 0 else left}, device_id_type=MESH_IDS)

    order = [(stream, part) for part in range(PARTS) for stream in range(2)]
    copies = []
    last = {}
    for stream, part in order:
        last[stream, part] = hop(stream, part, 0)
        last[stream, part].start()
        copies.append(last[stream, part])
    grad_step(0)
    for step in range(1, max(n, n_r) - 1):
        if step >= n - 1:
            if step < n_r - 1:
                grad_step(step)
            continue
        for stream, part in order:
            rows = pl.ds(part * half, half)
            last[stream, part].wait_recv()
            here = parts[stream][chunk_for(stream, step), rows].astype(jnp.float32)
            if step == 1:
                came = firsts[stream][rows].astype(jnp.float32)
            elif step <= WIDE_FROM:
                came = seconds[stream][step - 2, rows].astype(jnp.float32)
            else:
                came = recvs[stream][step - 1, rows]
            if step < WIDE_FROM:
                second_outs[stream][step - 1, rows] = (came + here).astype(second_outs[stream].dtype)
            else:
                sends[stream][step, rows] = came + here
            last[stream, part] = hop(stream, part, step)
            last[stream, part].start()
            copies.append(last[stream, part])
        if step < n_r - 1:
            grad_step(step)
    for stream, part in order:
        rows = pl.ds(part * half, half)
        last[stream, part].wait_recv()
        o_ref[stream, rows] = (
            recvs[stream][n - 2, rows] + parts[stream][me, rows].astype(jnp.float32)
        ).astype(o_ref.dtype)
    own = pl.ds(pl.multiple_of(rep_at(pos) * block, block), block)
    for stream, out in ((0, od_ref), (1, ou_ref)):
        grad_last[stream].wait_recv()
        out[...] = grecvs[stream][n_r - 2] + grads[stream][own]
    for copy in copies + grad_copies:
        copy.wait_send()


def ring_sum(first, second, grad_d, grad_u, n, n_r):
    _, rows, width = first.shape
    d_rows, d_cols = grad_d.shape
    block = d_rows // n_r
    return pl.pallas_call(
        functools.partial(ring_sum_kernel, n, n_r),
        out_shape=(
            jax.ShapeDtypeStruct((2, rows, width), first.dtype),
            jax.ShapeDtypeStruct((block, d_cols), grad_d.dtype),
            jax.ShapeDtypeStruct((block, d_cols), grad_u.dtype),
        ),
        in_specs=[pl.BlockSpec(memory_space=pltpu.VMEM)] * 4,
        out_specs=[pl.BlockSpec(memory_space=pltpu.VMEM)] * 3,
        scratch_shapes=[pltpu.VMEM((rows, width), first.dtype)] * 2
        + [pltpu.VMEM((WIDE_FROM - 1, rows, width), first.dtype)] * 4
        + [pltpu.VMEM((n - 1, rows, width), jnp.float32)] * 4
        + [pltpu.SemaphoreType.DMA((2, PARTS, n - 1)), pltpu.SemaphoreType.DMA((2, PARTS, n - 1))]
        + [pltpu.VMEM((n_r - 1, block, d_cols), jnp.float32)] * 4
        + [pltpu.SemaphoreType.DMA((2, n_r - 1)), pltpu.SemaphoreType.DMA((2, n_r - 1))],
        compiler_params=pltpu.CompilerParams(
            collective_id=1, has_side_effects=True, vmem_limit_bytes=44 * MIB),
    )(first, second, grad_d, grad_u)


def y_exchange_kernel(n_y, x_ref, o_ref, send_sem, recv_sem):
    me = lax.axis_index("ly")
    barrier = pltpu.get_barrier_semaphore()
    for k in range(1, n_y):
        pl.semaphore_signal(
            barrier, inc=1, device_id={"ly": lax.rem(me + k, n_y)}, device_id_type=MESH_IDS)
    pl.semaphore_wait(barrier, n_y - 1)

    def exchange(k, src, dst):
        return pltpu.make_async_remote_copy(
            src_ref=src, dst_ref=dst, send_sem=send_sem.at[k], recv_sem=recv_sem.at[k],
            device_id={"ly": lax.rem(me + k, n_y)}, device_id_type=MESH_IDS)

    copies = []
    for k in range(1, n_y):
        copy = exchange(k, x_ref.at[:, lax.rem(me + k, n_y)], o_ref.at[:, me])
        copy.start()
        copies.append(copy)
    o_ref[:, me] = x_ref[:, me]
    for k in range(1, n_y):
        exchange(k, x_ref.at[:, me], o_ref.at[:, lax.rem(me + n_y - k, n_y)]).wait_recv()
    for copy in copies:
        copy.wait_send()


def y_exchange(x, call_id):
    n_y = x.shape[1]
    return pl.pallas_call(
        functools.partial(y_exchange_kernel, n_y),
        out_shape=jax.ShapeDtypeStruct(x.shape, x.dtype),
        in_specs=[pl.BlockSpec(memory_space=pltpu.VMEM)],
        out_specs=pl.BlockSpec(memory_space=pltpu.VMEM),
        scratch_shapes=[pltpu.SemaphoreType.DMA((n_y,)), pltpu.SemaphoreType.DMA((n_y,))],
        compiler_params=pltpu.CompilerParams(
            collective_id=call_id, has_side_effects=True, vmem_limit_bytes=8 * MIB),
    )(x)


def per_device(tokens, grad_out, lang_ids, slot_ids, w_up, w_down_t):
    feature_width = tokens.shape[1]
    capacity = CAPACITY
    keep_mask = slot_ids < capacity
    target = jnp.where(keep_mask, lang_ids * capacity + slot_ids, MODULES * capacity)
    safe_slot = jnp.minimum(slot_ids, capacity - 1)
    token_scale = 1.0 / TOK_DEV

    def place(values):
        buffer = (
            jnp.zeros((MODULES * capacity, feature_width), values.dtype)
            .at[target]
            .set(values, mode="drop")
        )
        return buffer.reshape(MODULES, capacity, feature_width)

    n_z = lax.axis_size("lz")

    def dispatch(first, second):
        both = jnp.stack([place(first), place(second)])
        lanes = 128
        by_y = y_exchange(both.reshape(2, MODULES, -1, lanes), 2)
        every = ring_gather(by_y.reshape(2, -1, feature_width), n_z)
        every = every.reshape(2, -1, feature_width)
        return every[0], every[1]

    def give_back(first, second, grad_d, grad_u):
        summed, grad_d, grad_u = ring_sum(
            first.reshape(n_z, -1, feature_width), second.reshape(n_z, -1, feature_width),
            grad_d, grad_u, n_z, lax.axis_size("rep"))
        summed = summed.reshape(2, -1, capacity, feature_width)
        back = y_exchange(summed.reshape(2, MODULES, -1, 128), 3)
        back = back.reshape(2, MODULES, capacity, feature_width)
        return back[0], back[1], grad_d, grad_u

    def collect(returned):
        picked = returned[lang_ids, safe_slot]
        return jnp.where(keep_mask[:, None], picked, jnp.zeros_like(picked))

    flat_tokens, flat_grads = dispatch(tokens, grad_out)
    pre_flat = jnp.dot(flat_tokens, w_up, preferred_element_type=jnp.float32)
    hidden_flat = gelu_value(pre_flat).astype(jnp.bfloat16)
    partial_rows = lax.dot_general(
        hidden_flat, w_down_t, (((1,), (1,)), ((), ())), preferred_element_type=jnp.float32
    ).astype(jnp.bfloat16)
    grad_down = lax.dot_general(
        flat_grads, hidden_flat, (((0,), (0,)), ((), ())), preferred_element_type=jnp.float32
    ) * token_scale
    d_hidden = jnp.dot(flat_grads, w_down_t, preferred_element_type=jnp.float32)
    d_pre = (d_hidden * gelu_slope(pre_flat)).astype(jnp.bfloat16)
    grad_up = lax.dot_general(
        flat_tokens, d_pre, (((0,), (0,)), ((), ())), preferred_element_type=jnp.float32
    ) * token_scale
    dx_part = lax.dot_general(
        d_pre, w_up, (((1,), (1,)), ((), ())), preferred_element_type=jnp.float32
    ).astype(jnp.bfloat16)
    returned, dx_back, grad_down, grad_up = give_back(partial_rows, dx_part, grad_down, grad_up)
    return (collect(returned), collect(dx_back), grad_up, grad_down)


def solution(mesh):
    n_lang = mesh.shape["lang"]
    groups = n_lang // MODULES
    devices = mesh.devices.reshape(MODULES, groups, mesh.shape["rep"])
    split_mesh = Mesh(devices, ("ly", "lz", "rep"))
    rows = P(("ly", "lz", "rep"), None)
    ids = P(("ly", "lz", "rep"))
    cols = P(None, ("ly", "lz"))
    return jax.shard_map(
        per_device,
        mesh=split_mesh,
        in_specs=(rows, rows, ids, ids, cols, cols),
        out_specs=(rows, rows, P("rep", ("ly", "lz")), P("rep", ("ly", "lz"))),
        check_vma=False,
    )
```

```python
import functools

import jax
import jax.numpy as jnp
from jax import lax
from jax.experimental import pallas as pl
from jax.experimental.pallas import tpu as pltpu
from jax.sharding import Mesh
from jax.sharding import PartitionSpec as P

MODULES = 8
TOK_DEV = 128
CAPACITY = 18


INV_ROOT_TWO = 0.7071067811865476
INV_ROOT_TAU = 0.3989422804014327


def gelu_value(values):
    return 0.5 * values * (1.0 + lax.erf(values * INV_ROOT_TWO))


def gelu_slope(values):
    return (
        0.5 * (1.0 + lax.erf(values * INV_ROOT_TWO))
        + values * jnp.exp(-0.5 * values * values) * INV_ROOT_TAU
    )

MESH_IDS = pl.DeviceIdType.MESH
MIB = 1024 * 1024
PARTS = 3
WIDE_FROM = 4


def enter(n, others=()):
    me = lax.axis_index("lz")
    right, left = lax.rem(me + 1, n), lax.rem(me + n - 1, n)
    peers = [("lz", left), ("lz", right)] + list(others)
    barrier = pltpu.get_barrier_semaphore()
    for axis, neighbour in peers:
        pl.semaphore_signal(barrier, inc=1, device_id={axis: neighbour}, device_id_type=MESH_IDS)
    pl.semaphore_wait(barrier, len(peers))
    return me, right, left


def rep_ring(n_r):
    rep = lax.axis_index("rep")
    chips = n_r // 2
    x, core = rep // 2, lax.rem(rep, 2)
    pos = core * (x + 1) + (1 - core) * lax.rem(n_r - x, n_r)

    def rep_at(p):
        p = lax.rem(p + 2 * n_r, n_r)
        up = 1 - lax.rem(p + n_r - 1, n_r) // chips
        return 2 * (up * (p - 1) + (1 - up) * lax.rem(n_r - p, n_r)) + up

    return pos, rep_at


def ring_gather_kernel(n, x_ref, o_ref, send_sem, recv_sem):
    me, right, left = enter(n)
    half = x_ref.shape[1] // PARTS

    def hop(stream, part, step):
        rows = pl.ds(part * half, half)
        if stream == 0:
            slot, peer = lax.rem(me - step + n, n), right
        else:
            slot, peer = lax.rem(me + step, n), left
        src = x_ref.at[stream, rows] if step == 0 else o_ref.at[stream, slot, rows]
        return pltpu.make_async_remote_copy(
            src_ref=src, dst_ref=o_ref.at[stream, slot, rows],
            send_sem=send_sem.at[stream, part, step], recv_sem=recv_sem.at[stream, part, step],
            device_id={"lz": peer}, device_id_type=MESH_IDS)

    order = [(stream, part) for part in range(PARTS) for stream in range(2)]
    copies = []
    last = {}
    for key in order:
        last[key] = hop(*key, 0)
        last[key].start()
        copies.append(last[key])
    o_ref[0, me] = x_ref[0]
    o_ref[1, me] = x_ref[1]
    for step in range(1, n - 1):
        for key in order:
            last[key].wait_recv()
            last[key] = hop(*key, step)
            last[key].start()
            copies.append(last[key])
    for key in order:
        last[key].wait_recv()
    for copy in copies:
        copy.wait_send()


def ring_gather(x, n):
    two, rows, width = x.shape
    return pl.pallas_call(
        functools.partial(ring_gather_kernel, n),
        out_shape=jax.ShapeDtypeStruct((two, n, rows, width), x.dtype),
        in_specs=[pl.BlockSpec(memory_space=pltpu.VMEM)],
        out_specs=pl.BlockSpec(memory_space=pltpu.VMEM),
        scratch_shapes=[pltpu.SemaphoreType.DMA((2, PARTS, n - 1)), pltpu.SemaphoreType.DMA((2, PARTS, n - 1))],
        compiler_params=pltpu.CompilerParams(
            collective_id=0, has_side_effects=True, vmem_limit_bytes=16 * MIB),
    )(x)


def ring_sum_kernel(n, n_r, pa_ref, pb_ref, gd_ref, gu_ref, o_ref, od_ref, ou_ref, first_r, first_l,
                    second_out_r, second_out_l, second_r, second_l,
                    send_r, send_l, recv_r, recv_l, send_sem, recv_sem,
                    gsend_f, gsend_b, grecv_f, grecv_b, gsend_sem, grecv_sem):
    pos, rep_at = rep_ring(n_r)
    ahead, behind = rep_at(pos + 1), rep_at(pos - 1)
    me, right, left = enter(n, [("rep", ahead), ("rep", behind)])
    block = od_ref.shape[0]
    grads = (gd_ref, gu_ref)
    gsends = (gsend_f, gsend_b)
    grecvs = (grecv_f, grecv_b)

    def grad_rows(stream, step):
        dest = pos - 1 - step if stream == 0 else pos + 1 + step
        return pl.ds(pl.multiple_of(rep_at(dest) * block, block), block)

    def grad_hop(stream, step):
        if step == 0:
            src = grads[stream].at[grad_rows(stream, 0)]
        else:
            src = gsends[stream].at[step]
        return pltpu.make_async_remote_copy(
            src_ref=src, dst_ref=grecvs[stream].at[step],
            send_sem=gsend_sem.at[stream, step], recv_sem=grecv_sem.at[stream, step],
            device_id={"rep": ahead if stream == 0 else behind}, device_id_type=MESH_IDS)

    grad_copies = []
    grad_last = {}

    def grad_step(step):
        for stream in range(2):
            if step > 0:
                grad_last[stream].wait_recv()
                gsends[stream][step] = grecvs[stream][step - 1] + grads[stream][grad_rows(stream, step)]
            grad_last[stream] = grad_hop(stream, step)
            grad_last[stream].start()
            grad_copies.append(grad_last[stream])

    half = pa_ref.shape[1] // PARTS
    parts = (pa_ref, pb_ref)
    sends = (send_r, send_l)
    recvs = (recv_r, recv_l)

    def chunk_for(stream, step):
        if stream == 0:
            return lax.rem(me + 2 * n - 1 - step, n)
        return lax.rem(me + 1 + step, n)

    firsts = (first_r, first_l)
    second_outs = (second_out_r, second_out_l)
    seconds = (second_r, second_l)

    def hop(stream, part, step):
        rows = pl.ds(part * half, half)
        if step == 0:
            src = parts[stream].at[chunk_for(stream, 0), rows]
            dst = firsts[stream].at[rows]
        elif step < WIDE_FROM:
            src = second_outs[stream].at[step - 1, rows]
            dst = seconds[stream].at[step - 1, rows]
        else:
            src, dst = sends[stream].at[step, rows], recvs[stream].at[step, rows]
        return pltpu.make_async_remote_copy(
            src_ref=src, dst_ref=dst,
            send_sem=send_sem.at[stream, part, step], recv_sem=recv_sem.at[stream, part, step],
            device_id={"lz": right if stream == 0 else left}, device_id_type=MESH_IDS)

    order = [(stream, part) for part in range(PARTS) for stream in range(2)]
    copies = []
    last = {}
    for stream, part in order:
        last[stream, part] = hop(stream, part, 0)
        last[stream, part].start()
        copies.append(last[stream, part])
    grad_step(0)
    for step in range(1, max(n, n_r) - 1):
        if step >= n - 1:
            if step < n_r - 1:
                grad_step(step)
            continue
        for stream, part in order:
            rows = pl.ds(part * half, half)
            last[stream, part].wait_recv()
            here = parts[stream][chunk_for(stream, step), rows].astype(jnp.float32)
            if step == 1:
                came = firsts[stream][rows].astype(jnp.float32)
            elif step <= WIDE_FROM:
                came = seconds[stream][step - 2, rows].astype(jnp.float32)
            else:
                came = recvs[stream][step - 1, rows]
            if step < WIDE_FROM:
                second_outs[stream][step - 1, rows] = (came + here).astype(second_outs[stream].dtype)
            else:
                sends[stream][step, rows] = came + here
            last[stream, part] = hop(stream, part, step)
            last[stream, part].start()
            copies.append(last[stream, part])
        if step < n_r - 1:
            grad_step(step)
    for stream, part in order:
        rows = pl.ds(part * half, half)
        last[stream, part].wait_recv()
        o_ref[stream, rows] = (
            recvs[stream][n - 2, rows] + parts[stream][me, rows].astype(jnp.float32)
        ).astype(o_ref.dtype)
    own = pl.ds(pl.multiple_of(rep_at(pos) * block, block), block)
    for stream, out in ((0, od_ref), (1, ou_ref)):
        grad_last[stream].wait_recv()
        out[...] = grecvs[stream][n_r - 2] + grads[stream][own]
    for copy in copies + grad_copies:
        copy.wait_send()


def ring_sum(first, second, grad_d, grad_u, n, n_r):
    _, rows, width = first.shape
    d_rows, d_cols = grad_d.shape
    block = d_rows // n_r
    return pl.pallas_call(
        functools.partial(ring_sum_kernel, n, n_r),
        out_shape=(
            jax.ShapeDtypeStruct((2, rows, width), first.dtype),
            jax.ShapeDtypeStruct((block, d_cols), grad_d.dtype),
            jax.ShapeDtypeStruct((block, d_cols), grad_u.dtype),
        ),
        in_specs=[pl.BlockSpec(memory_space=pltpu.VMEM)] * 4,
        out_specs=[pl.BlockSpec(memory_space=pltpu.VMEM)] * 3,
        scratch_shapes=[pltpu.VMEM((rows, width), first.dtype)] * 2
        + [pltpu.VMEM((WIDE_FROM - 1, rows, width), first.dtype)] * 4
        + [pltpu.VMEM((n - 1, rows, width), jnp.float32)] * 4
        + [pltpu.SemaphoreType.DMA((2, PARTS, n - 1)), pltpu.SemaphoreType.DMA((2, PARTS, n - 1))]
        + [pltpu.VMEM((n_r - 1, block, d_cols), jnp.float32)] * 4
        + [pltpu.SemaphoreType.DMA((2, n_r - 1)), pltpu.SemaphoreType.DMA((2, n_r - 1))],
        compiler_params=pltpu.CompilerParams(
            collective_id=1, has_side_effects=True, vmem_limit_bytes=44 * MIB),
    )(first, second, grad_d, grad_u)


def y_exchange_kernel(n_y, x_ref, o_ref, send_sem, recv_sem):
    me = lax.axis_index("ly")
    barrier = pltpu.get_barrier_semaphore()
    for k in range(1, n_y):
        pl.semaphore_signal(
            barrier, inc=1, device_id={"ly": lax.rem(me + k, n_y)}, device_id_type=MESH_IDS)
    pl.semaphore_wait(barrier, n_y - 1)

    def exchange(k, src, dst):
        return pltpu.make_async_remote_copy(
            src_ref=src, dst_ref=dst, send_sem=send_sem.at[k], recv_sem=recv_sem.at[k],
            device_id={"ly": lax.rem(me + k, n_y)}, device_id_type=MESH_IDS)

    copies = []
    for k in range(1, n_y):
        copy = exchange(k, x_ref.at[:, lax.rem(me + k, n_y)], o_ref.at[:, me])
        copy.start()
        copies.append(copy)
    o_ref[:, me] = x_ref[:, me]
    for k in range(1, n_y):
        exchange(k, x_ref.at[:, me], o_ref.at[:, lax.rem(me + n_y - k, n_y)]).wait_recv()
    for copy in copies:
        copy.wait_send()


def y_exchange(x, call_id):
    n_y = x.shape[1]
    return pl.pallas_call(
        functools.partial(y_exchange_kernel, n_y),
        out_shape=jax.ShapeDtypeStruct(x.shape, x.dtype),
        in_specs=[pl.BlockSpec(memory_space=pltpu.VMEM)],
        out_specs=pl.BlockSpec(memory_space=pltpu.VMEM),
        scratch_shapes=[pltpu.SemaphoreType.DMA((n_y,)), pltpu.SemaphoreType.DMA((n_y,))],
        compiler_params=pltpu.CompilerParams(
            collective_id=call_id, has_side_effects=True, vmem_limit_bytes=8 * MIB),
    )(x)


def per_device(tokens, grad_out, lang_ids, slot_ids, w_up, w_down_t):
    feature_width = tokens.shape[1]
    capacity = CAPACITY
    keep_mask = slot_ids < capacity
    target = jnp.where(keep_mask, lang_ids * capacity + slot_ids, MODULES * capacity)
    safe_slot = jnp.minimum(slot_ids, capacity - 1)
    token_scale = 1.0 / TOK_DEV

    def place(values):
        buffer = (
            jnp.zeros((MODULES * capacity, feature_width), values.dtype)
            .at[target]
            .set(values, mode="drop")
        )
        return buffer.reshape(MODULES, capacity, feature_width)

    n_z = lax.axis_size("lz")

    def dispatch(first, second):
        both = jnp.stack([place(first), place(second)])
        lanes = 128
        by_y = y_exchange(both.reshape(2, MODULES, -1, lanes), 2)
        every = ring_gather(by_y.reshape(2, -1, feature_width), n_z)
        every = every.reshape(2, -1, feature_width)
        return every[0], every[1]

    def give_back(first, second, grad_d, grad_u):
        summed, grad_d, grad_u = ring_sum(
            first.reshape(n_z, -1, feature_width), second.reshape(n_z, -1, feature_width),
            grad_d, grad_u, n_z, lax.axis_size("rep"))
        summed = summed.reshape(2, -1, capacity, feature_width)
        back = y_exchange(summed.reshape(2, MODULES, -1, 128), 3)
        back = back.reshape(2, MODULES, capacity, feature_width)
        return back[0], back[1], grad_d, grad_u

    def collect(returned):
        picked = returned[lang_ids, safe_slot]
        return jnp.where(keep_mask[:, None], picked, jnp.zeros_like(picked))

    flat_tokens, flat_grads = dispatch(tokens, grad_out)
    pre_flat = jnp.dot(flat_tokens, w_up, preferred_element_type=jnp.float32)
    hidden_flat = gelu_value(pre_flat).astype(jnp.bfloat16)
    partial_rows = lax.dot_general(
        hidden_flat, w_down_t, (((1,), (1,)), ((), ())), preferred_element_type=jnp.float32
    ).astype(jnp.bfloat16)
    grad_down = lax.dot_general(
        flat_grads, hidden_flat, (((0,), (0,)), ((), ())), preferred_element_type=jnp.float32
    ) * token_scale
    d_hidden = jnp.dot(flat_grads, w_down_t, preferred_element_type=jnp.float32)
    d_pre = (d_hidden * gelu_slope(pre_flat)).astype(jnp.bfloat16)
    grad_up = lax.dot_general(
        flat_tokens, d_pre, (((0,), (0,)), ((), ())), preferred_element_type=jnp.float32
    ) * token_scale
    dx_part = lax.dot_general(
        d_pre, w_up, (((1,), (1,)), ((), ())), preferred_element_type=jnp.float32
    ).astype(jnp.bfloat16)
    returned, dx_back, grad_down, grad_up = give_back(partial_rows, dx_part, grad_down, grad_up)
    return (collect(returned), collect(dx_back), grad_up, grad_down)


def solution(mesh):
    n_lang = mesh.shape["lang"]
    groups = n_lang // MODULES
    devices = mesh.devices.reshape(MODULES, groups, mesh.shape["rep"])
    split_mesh = Mesh(devices, ("ly", "lz", "rep"))
    rows = P(("ly", "lz", "rep"), None)
    ids = P(("ly", "lz", "rep"))
    cols = P(None, ("ly", "lz"))
    return jax.shard_map(
        per_device,
        mesh=split_mesh,
        in_specs=(rows, rows, ids, ids, cols, cols),
        out_specs=(rows, rows, P("rep", ("ly", "lz")), P("rep", ("ly", "lz"))),
        check_vma=False,
    )
```
